128 devices in a mesh: segment: 4 (over x_lo, core), dp: 32 (over z, y, x_hi).
Axes of the slice: x: 4 (x_hi: 2, x_lo: 2; x = x_hi * 2 + x_lo), y: 4, z: 4, core: 2. Of those that a mesh axis runs over, the one named last changes fastest.
Arguments:
- latents: bfloat16 [2, 4096, 1280], P(None, 'dp'), may hold values from -6 to 6
- cotangent: bfloat16 [2, 4096, 1280], P(None, 'dp'), may hold values from -6 to 6
- timesteps: int32 [2, 32], P(None, 'dp'), may hold values from 0 to 999
- time_table: bfloat16 [4, 1000, 1280], P('segment'), may hold values from -3 to 3
- w_in: bfloat16 [4, 1280, 1280], P('segment'), may hold values from -0.15625 to 0.15625
- w_out: bfloat16 [4, 1280, 1280], P('segment'), may hold values from -0.15625 to 0.15625
- w_skip: bfloat16 [4, 1280, 1280], P('segment'), may hold values from -0.15625 to 0.15625
Outputs:
- phase_out: bfloat16 [4, 2, 4096, 1280], P('segment', None, 'dp')
- input_grads: bfloat16 [4, 2, 4096, 1280], P('segment', None, 'dp')
- grad_w_in: float32 [4, 1280, 1280], P('segment', 'dp')
- grad_w_out: float32 [4, 1280, 1280], P('segment', 'dp')
- grad_w_skip: float32 [4, 1280, 1280], P('segment', 'dp')
The draws below stay inside these ranges and needn't reach their ends.
All inputs are finite; a program needn't handle non-finite values.
Results may differ from the reference program's by a relative error of at most 0.028.
Values may be sent and summed in bfloat16 or wider, within the bound.
A program may use at most 128 MiB of HBM per device.

```python
import jax
import jax.numpy as jnp

C = 1280
TSTEPS = 1000
MICRO = 2
ROWS = 128
SEGMENTS = 4
SAMPLES = 32
ROWS_ALL = 4096


def with_ends(array, stream_key, least, high):
    longest = array.shape.index(max(array.shape))
    spots = []
    for shift in (0, 1):
        where = [jax.random.randint(jax.random.fold_in(stream_key, axis), (), 0, length) for axis, length in enumerate(array.shape)]
        where[longest] = (where[longest] + shift) % array.shape[longest]
        spots.append(tuple(where))
    return array.at[spots[0]].set(least).at[spots[1]].set(high)


def block_scale(key, dims, pieces, low, top_value):
    loudness = 1.0
    for position, parts in pieces:
        draws = jax.random.uniform(jax.random.fold_in(jax.random.fold_in(key, 6), position), (parts,), jnp.float32, low / len(pieces), top_value / len(pieces))
        loudness = loudness * jnp.repeat(jnp.exp(draws), dims[position] // parts).reshape((-1,) + (1,) * (len(dims) - 1 - position))
    return loudness


def scatter_about(stream_key, extent, scale, limit, pieces=(), dtype=jnp.bfloat16):
    entries = scale * jax.random.normal(stream_key, extent, jnp.float32)
    if pieces:
        entries = entries * block_scale(stream_key, extent, pieces, -0.22, 0.18)
    return jnp.clip(entries, -limit, limit).astype(dtype)


def setup_inputs(seed: int = 0) -> dict:
    splits = jax.random.split(jax.random.key(seed), 8)
    latents = scatter_about(splits[0], (MICRO, ROWS_ALL, C), 1.0, 6.0, ((1, 32),))
    cotangent = scatter_about(splits[1], (MICRO, ROWS_ALL, C), 1.0, 6.0, ((1, 32),))
    timesteps = with_ends(jax.random.randint(splits[2], (MICRO, SAMPLES), 0, TSTEPS), jax.random.fold_in(splits[2], 1), 0, TSTEPS - 1).astype(jnp.int32)
    time_table = scatter_about(splits[3], (SEGMENTS, TSTEPS, C), 0.5, 3.0, ((0, 4),))
    w_in = scatter_about(splits[4], (SEGMENTS, C, C), C ** -0.5, 0.15625, ((0, 4),))
    w_out = scatter_about(splits[5], (SEGMENTS, C, C), C ** -0.5, 0.15625, ((0, 4),))
    w_skip = scatter_about(splits[6], (SEGMENTS, C, C), C ** -0.5, 0.15625, ((0, 4),))
    return dict(latents=latents, cotangent=cotangent, timesteps=timesteps, time_table=time_table, w_in=w_in, w_out=w_out, w_skip=w_skip)


def silu_grad(pre):
    sig = jax.nn.sigmoid(pre)
    return sig * (1.0 + pre * (1.0 - sig))

def reference(latents, cotangent, timesteps, time_table, w_in, w_out, w_skip):
    outs_all = [[], [], [], []]
    grads_all = [[], [], [], []]
    width = w_in.shape[1]
    acc_first = [jnp.zeros((width, width), jnp.float32) for _ in range(4)]
    acc_second = [jnp.zeros((width, width), jnp.float32) for _ in range(4)]
    acc_side = [jnp.zeros((width, width), jnp.float32) for _ in range(4)]
    for micro_id in range(MICRO):
        action = latents[micro_id]
        skips = []
        saved = []
        for phase in range(4):
            bias = jnp.repeat(time_table[phase][timesteps[micro_id]].astype(jnp.float32), ROWS, axis=0)
            pre = jnp.dot(action, w_in[phase], preferred_element_type=jnp.float32) + bias
            if phase >= 2:
                side = skips[3 - phase]
                pre = pre + jnp.dot(side, w_skip[phase], preferred_element_type=jnp.float32)
            gated = jax.nn.silu(pre).astype(jnp.bfloat16)
            output = (action.astype(jnp.float32) + jnp.dot(gated, w_out[phase], preferred_element_type=jnp.float32)).astype(jnp.bfloat16)
            if phase < 2:
                skips.append(jnp.dot(output, w_skip[phase], preferred_element_type=jnp.float32).astype(jnp.bfloat16))
                left = output
            else:
                left = side
            saved.append((action, pre, gated, left))
            outs_all[phase].append(output)
            action = output
        upstream = cotangent[micro_id]
        dskips = [None, None]
        for phase in [3, 2, 1, 0]:
            action, pre, gated, left = saved[phase]
            if phase >= 2:
                total = upstream
            else:
                total = (upstream.astype(jnp.float32) + jnp.dot(dskips[phase], w_skip[phase].T, preferred_element_type=jnp.float32)).astype(jnp.bfloat16)
            d_pre = (jnp.dot(total, w_out[phase].T, preferred_element_type=jnp.float32) * silu_grad(pre)).astype(jnp.bfloat16)
            if phase >= 2:
                dskips[3 - phase] = jnp.dot(d_pre, w_skip[phase].T, preferred_element_type=jnp.float32).astype(jnp.bfloat16)
                right = d_pre
            else:
                right = dskips[phase]
            acc_first[phase] = acc_first[phase] + jnp.dot(action.T, d_pre, preferred_element_type=jnp.float32)
            acc_second[phase] = acc_second[phase] + jnp.dot(gated.T, total, preferred_element_type=jnp.float32)
            acc_side[phase] = acc_side[phase] + jnp.dot(left.T, right, preferred_element_type=jnp.float32)
            d_in = (total.astype(jnp.float32) + jnp.dot(d_pre, w_in[phase].T, preferred_element_type=jnp.float32)).astype(jnp.bfloat16)
            grads_all[phase].append(d_in)
            upstream = d_in
    phase_out = jnp.stack([jnp.stack(outs_all[phase]) for phase in range(4)])
    input_grads = jnp.stack([jnp.stack(grads_all[phase]) for phase in range(4)])
    return (phase_out, input_grads, jnp.stack(acc_first), jnp.stack(acc_second), jnp.stack(acc_side))
```

```python
import jax
import jax.numpy as jnp
from jax import lax
from jax.experimental import pallas as pl
from jax.experimental.pallas import tpu as pltpu
from jax.sharding import PartitionSpec as P

MESH = pl.DeviceIdType.MESH
F32 = jnp.float32
BF16 = jnp.bfloat16
C = 1280
R = 128
TILE = 256
NT = (((1,), (1,)), ((), ()))
SPLITS = (
    ((0, 384, 0, 1), (384, 256, 0, -1), (640, 256, 1, 1), (896, 384, 1, -1)),
    ((0, 256, 0, 1), (256, 384, 0, -1), (640, 384, 1, 1), (1024, 256, 1, -1)),
    ((0, 384, 0, 1), (384, 256, 0, -1), (640, 256, 1, 1), (896, 384, 1, -1)),
)
BLOCKS = tuple((k, n, *block) for k in range(3) for n, block in enumerate(SPLITS[k]))


def kernel(
    lat, cot, bias, w_in, w_out, w_skip,
    po, gi, g_in, g_out, g_skip,
    w1, w2, w3, x, up, sk, dk, pre, gat, tot, dpre, lt, grads, r1, r2, r3, s1, q1, q2, q3, xs, xr,
    wsem, x_s, x_r, sk_s, sk_r, up_s, up_r, dk_s, dk_r, rs_s, rs_r, xh_s, xh_r,
):
    s = lax.axis_index("segment")
    dp = lax.axis_index("dp")
    z = dp // 8
    y = (dp // 2) % 4
    xh = dp % 2

    def along(axis, by):
        if axis == 0:
            return ((z + by + 4) % 4) * 8 + y * 2 + xh
        return z * 8 + ((y + by + 4) % 4) * 2 + xh

    partner = z * 8 + y * 2 + (1 - xh)
    loads = [
        pltpu.make_async_copy(src, dst, wsem.at[n])
        for n, (src, dst) in enumerate(((w_in, w1), (w_out, w2), (w_skip, w3)))
    ]
    x_load = pltpu.make_async_copy(lat, x, x_r.at[2])
    up_load = pltpu.make_async_copy(cot, up, up_r.at[2])

    @pl.when(s == 0)
    def _():
        x_load.start()

    for load in loads:
        load.start()

    @pl.when(s == 3)
    def _():
        up_load.start()

    barrier = pltpu.get_barrier_semaphore()
    for by in (1, 2, 3):
        pl.semaphore_signal(barrier, inc=1, device_id={"segment": (s + by) % 4}, device_id_type=MESH)
    for other in (along(0, 1), along(0, -1), along(1, 1), along(1, -1), partner):
        pl.semaphore_signal(barrier, inc=1, device_id={"dp": other}, device_id_type=MESH)
    pl.semaphore_wait(barrier, 8)

    def hand(buf, dst, m, send, recv, to):
        rows = pl.ds(pl.multiple_of(m * R, R), R)
        return pltpu.make_async_remote_copy(
            src_ref=buf.at[rows], dst_ref=dst.at[rows], send_sem=send.at[m], recv_sem=recv.at[m],
            device_id={"segment": to}, device_id_type=MESH,
        )

    def send_x(m):
        return hand(po, x, m, x_s, x_r, (s + 1) % 4)

    def send_sk(m):
        return hand(sk, sk, m, sk_s, sk_r, 3 - s)

    def send_up(m):
        return hand(gi, up, m, up_s, up_r, (s + 3) % 4)

    def send_dk(m):
        return hand(dk, dk, m, dk_s, dk_r, 3 - s)

    columns = [pl.ds(n * TILE, TILE) for n in range(C // TILE)]
    on3 = s // 3

    @pl.loop(0, 4)
    def _(i):
        kind = on3 * (i % 2) + (1 - on3) * (i // 2)
        m = on3 * (i // 2) + (1 - on3) * (i % 2)
        rows = pl.ds(pl.multiple_of(m * R, R), R)

        @pl.when(kind == 0)
        def _():
            @pl.when((s == 0) & (m == 0))
            def _():
                x_load.wait()

            @pl.when(s > 0)
            def _():
                send_x(m).wait_recv()

            @pl.when(i == 0)
            def _():
                loads[0].wait()

            for n in columns:
                pre[rows, n] = (
                    jnp.dot(x[rows, :], w1[:, n], preferred_element_type=F32) + bias[m, :, n]
                )

            @pl.when(i == 0)
            def _():
                loads[1].wait()
                loads[2].wait()

            @pl.when(s >= 2)
            def _():
                send_sk(m).wait_recv()
                for n in columns:
                    pre[rows, n] += jnp.dot(sk[rows, :], w3[:, n], preferred_element_type=F32)

            for n in columns:
                v = pre[rows, n]
                g = 1.0 / (1.0 + jnp.exp(-v))
                gat[rows, n] = (v * g).astype(BF16)
                pre[rows, n] = g * (1.0 + v * (1.0 - g))
            for n in columns:
                po[rows, n] = (
                    x[rows, n].astype(F32)
                    + jnp.dot(gat[rows, :], w2[:, n], preferred_element_type=F32)
                ).astype(BF16)

            @pl.when(s < 3)
            def _():
                send_x(m).start()

            @pl.when(s < 2)
            def _():
                for n in columns:
                    sk[rows, n] = jnp.dot(
                        po[rows, :], w3[:, n], preferred_element_type=F32
                    ).astype(BF16)
                send_sk(m).start()

        @pl.when(kind == 1)
        def _():
            @pl.when((s == 3) & (m == 0))
            def _():
                up_load.wait()

            @pl.when(s < 3)
            def _():
                send_up(m).wait_recv()

            @pl.when(s < 2)
            def _():
                send_dk(m).wait_recv()
                for n in columns:
                    tot[rows, n] = (
                        up[rows, n].astype(F32)
                        + lax.dot_general(dk[rows, :], w3[n, :], NT, preferred_element_type=F32)
                    ).astype(BF16)

            @pl.when(s >= 2)
            def _():
                tot[rows, :] = up[rows, :]

            for n in columns:
                dpre[rows, n] = (
                    lax.dot_general(tot[rows, :], w2[n, :], NT, preferred_element_type=F32)
                    * pre[rows, n]
                ).astype(BF16)
            for n in columns:
                gi[rows, n] = (
                    tot[rows, n].astype(F32)
                    + lax.dot_general(dpre[rows, :], w1[n, :], NT, preferred_element_type=F32)
                ).astype(BF16)

            @pl.when(s > 0)
            def _():
                send_up(m).start()

            @pl.when(s >= 2)
            def _():
                for n in columns:
                    dk[rows, n] = lax.dot_general(
                        dpre[rows, :], w3[n, :], NT, preferred_element_type=F32
                    ).astype(BF16)
                send_dk(m).start()

        @pl.when(kind == on3)
        def _():
            for n in columns:
                lt[0, n, rows] = x[rows, n].T
                lt[1, n, rows] = gat[rows, n].T

            @pl.when(s < 2)
            def _():
                for n in columns:
                    lt[2, n, rows] = po[rows, n].T

            @pl.when(s >= 2)
            def _():
                for n in columns:
                    lt[2, n, rows] = sk[rows, n].T

    def ring(stage, msg, block, src, dst, axis, by):
        n = block[0] * 4 + block[1]
        return pltpu.make_async_remote_copy(
            src_ref=src, dst_ref=dst, send_sem=rs_s.at[stage, msg, n], recv_sem=rs_r.at[stage, msg, n],
            device_id={"dp": along(axis, by)}, device_id_type=MESH,
        )

    def piece(block, pos):
        k, _, col, width, colour, _ = block
        cols = pl.ds(col, width)
        if colour == 0:
            return grads.at[k, pos % 4, :, :, cols]
        return grads.at[k, :, pos % 4, :, cols]

    def first(block, msg):
        k, _, col, width, colour, by = block
        cols = pl.ds(col, width)
        pos = (z, y)[colour]
        if msg == 0:
            return ring(0, 0, block, piece(block, pos + 2), r1.at[k, :, :, cols], colour, by)
        if msg == 1:
            return ring(0, 1, block, r1.at[k, :, :, cols], r2.at[k, :, :, cols], colour, by)
        return ring(0, 2, block, piece(block, pos - by + 4), r3.at[k, :, :, cols], colour, -by)

    def second(block, msg):
        k, _, col, width, colour, by = block
        cols = pl.ds(col, width)
        pos = (y, z)[colour]
        axis = 1 - colour
        if msg == 0:
            return ring(1, 0, block, s1.at[k, (pos + 2) % 4, :, cols], q1.at[k, :, cols], axis, by)
        if msg == 1:
            return ring(1, 1, block, q1.at[k, :, cols], q2.at[k, :, cols], axis, by)
        return ring(1, 2, block, s1.at[k, (pos - by + 4) % 4, :, cols], q3.at[k, :, cols], axis, -by)

    def product(k, right):
        @pl.loop(0, 4)
        def _(zp):
            left = lt[k, pl.ds(pl.multiple_of(zp * 320, 320), 320), :]
            for n in columns:
                acc = jnp.dot(left, right[:, n], preferred_element_type=F32).astype(BF16)
                for yp in range(4):
                    grads[k, zp, yp, :, n] = acc[yp * 80 : (yp + 1) * 80]

    for k in (1, 2, 0):
        if k == 2:

            @pl.when(s < 2)
            def _():
                product(2, dk)

            @pl.when(s >= 2)
            def _():
                product(2, dpre)
        else:
            product(k, (dpre, tot)[k])
        for block in BLOCKS[4 * k : 4 * k + 4]:
            first(block, 0).start()
            first(block, 2).start()
    order = BLOCKS[4:12] + BLOCKS[:4]
    for block in order:
        k, _, col, width, colour, by = block
        cols = pl.ds(col, width)
        first(block, 0).wait_recv()
        pos = (z, y)[colour] + by + 4
        r1[k, :, :, cols] = (
            r1[k, :, :, cols].astype(F32) + piece(block, pos)[...].astype(F32)
        ).astype(BF16)
        first(block, 1).start()
    for block in order:
        k, _, col, width, colour, by = block
        cols = pl.ds(col, width)
        first(block, 1).wait_recv()
        first(block, 2).wait_recv()
        s1[k, :, :, cols] = (
            piece(block, (z, y)[colour])[...].astype(F32)
            + r2[k, :, :, cols].astype(F32)
            + r3[k, :, :, cols].astype(F32)
        ).astype(BF16)
        second(block, 0).start()
        second(block, 2).start()
    for block in order:
        k, _, col, width, colour, by = block
        cols = pl.ds(col, width)
        second(block, 0).wait_recv()
        pos = ((y, z)[colour] + by + 4) % 4
        q1[k, :, cols] = (q1[k, :, cols].astype(F32) + s1[k, pos, :, cols].astype(F32)).astype(BF16)
        second(block, 1).start()

    def pair(k):
        return pltpu.make_async_remote_copy(
            src_ref=xs.at[k, 1 - xh], dst_ref=xr.at[k], send_sem=xh_s.at[k], recv_sem=xh_r.at[k],
            device_id={"dp": partner}, device_id_type=MESH,
        )

    for block in order:
        k, last, col, width, colour, by = block
        cols = pl.ds(col, width)
        second(block, 1).wait_recv()
        second(block, 2).wait_recv()
        part = (
            s1[k, (y, z)[colour], :, cols].astype(F32)
            + q2[k, :, cols].astype(F32)
            + q3[k, :, cols].astype(F32)
        )
        xs[k, 0, :, cols] = part[:40].astype(BF16)
        xs[k, 1, :, cols] = part[40:].astype(BF16)
        if last == 3:
            pair(k).start()
    for k in (1, 2, 0):
        pair(k).wait_recv()
        (g_in, g_out, g_skip)[k][...] = xs[k, xh].astype(F32) + xr[k].astype(F32)
    for block in order:
        for msg in range(3):
            first(block, msg).wait_send()
            second(block, msg).wait_send()
    for k in range(3):
        pair(k).wait_send()
    for m in range(2):

        @pl.when(s < 3)
        def _():
            send_x(m).wait_send()

        @pl.when(s < 2)
        def _():
            send_sk(m).wait_send()

        @pl.when(s > 0)
        def _():
            send_up(m).wait_send()

        @pl.when(s >= 2)
        def _():
            send_dk(m).wait_send()


def body(latents, cotangent, timesteps, time_table, w_in, w_out, w_skip):
    rows = 2 * R
    bias = time_table[0][timesteps[:, 0]].astype(F32)[:, None, :]
    vmem = pl.BlockSpec(memory_space=pltpu.VMEM)
    hbm = pl.BlockSpec(memory_space=pl.ANY)
    act = pltpu.VMEM((rows, C), BF16)
    weight = pltpu.VMEM((C, C), BF16)
    quarter = pltpu.VMEM((3, 4, 80, C), BF16)
    sixteenth = pltpu.VMEM((3, 80, C), BF16)
    dma = pltpu.SemaphoreType.DMA
    out_act = jax.ShapeDtypeStruct((rows, C), BF16)
    out_grad = jax.ShapeDtypeStruct((40, C), F32)
    po, gi, g_in, g_out, g_skip = pl.pallas_call(
        kernel,
        name="window",
        out_shape=(out_act, out_act, out_grad, out_grad, out_grad),
        in_specs=[hbm, hbm, vmem, hbm, hbm, hbm],
        out_specs=[vmem] * 5,
        scratch_shapes=[
            weight, weight, weight,
            act, act, act, act,
            pltpu.VMEM((rows, C), F32),
            act, act, act,
            pltpu.VMEM((3, C, rows), BF16),
            pltpu.VMEM((3, 4, 4, 80, C), BF16),
            quarter, quarter, quarter, quarter,
            sixteenth, sixteenth, sixteenth,
            pltpu.VMEM((3, 2, 40, C), BF16),
            pltpu.VMEM((3, 40, C), BF16),
            dma((3,)),
            dma((2,)), dma((3,)),
            dma((2,)), dma((2,)),
            dma((2,)), dma((3,)),
            dma((2,)), dma((2,)),
            dma((2, 3, 12)), dma((2, 3, 12)),
            dma((3,)), dma((3,)),
        ],
        compiler_params=pltpu.CompilerParams(
            collective_id=0, has_side_effects=True, vmem_limit_bytes=60 * 1024 * 1024
        ),
    )(
        latents.reshape(rows, C), cotangent.reshape(rows, C), bias,
        w_in.reshape(C, C), w_out.reshape(C, C), w_skip.reshape(C, C),
    )
    return (
        po.reshape(1, 2, R, C),
        gi.reshape(1, 2, R, C),
        g_in[None],
        g_out[None],
        g_skip[None],
    )


def solution(mesh):
    in_specs = (
        P(None, "dp", None),
        P(None, "dp", None),
        P(None, "dp"),
        P("segment", None, None),
        P("segment", None, None),
        P("segment", None, None),
        P("segment", None, None),
    )
    out_specs = (
        P("segment", None, "dp", None),
        P("segment", None, "dp", None),
        P("segment", "dp", None),
        P("segment", "dp", None),
        P("segment", "dp", None),
    )
    return jax.shard_map(body, mesh=mesh, in_specs=in_specs, out_specs=out_specs, check_vma=False)
```

```python
import jax
import jax.numpy as jnp
from jax import lax
from jax.experimental import pallas as pl
from jax.experimental.pallas import tpu as pltpu
from jax.sharding import PartitionSpec as P

MESH = pl.DeviceIdType.MESH
F32 = jnp.float32
BF16 = jnp.bfloat16
C = 1280
R = 128
TILE = 256
NT = (((1,), (1,)), ((), ()))
SPLITS = (
    ((0, 384, 0, 1), (384, 256, 0, -1), (640, 256, 1, 1), (896, 384, 1, -1)),
    ((0, 256, 0, 1), (256, 384, 0, -1), (640, 384, 1, 1), (1024, 256, 1, -1)),
    ((0, 384, 0, 1), (384, 256, 0, -1), (640, 256, 1, 1), (896, 384, 1, -1)),
)
BLOCKS = tuple((k, n, *block) for k in range(3) for n, block in enumerate(SPLITS[k]))


def kernel(
    lat, cot, steps, table, w_in, w_out, w_skip,
    po, gi, g_in, g_out, g_skip,
    w1, w2, w3, bias, x, up, sk, dk, pre, gat, tot, dpre, lt, grads, r1, r2, r3, s1, q1, q2, q3, xs, xr,
    wsem, turn, x_s, x_r, sk_s, sk_r, up_s, up_r, dk_s, dk_r, rs_s, rs_r, xh_s, xh_r,
):
    s = lax.axis_index("segment")
    dp = lax.axis_index("dp")
    z = dp // 8
    y = (dp // 2) % 4
    xh = dp % 2

    def along(axis, by):
        if axis == 0:
            return ((z + by + 4) % 4) * 8 + y * 2 + xh
        return z * 8 + ((y + by + 4) % 4) * 2 + xh

    partner = z * 8 + y * 2 + (1 - xh)
    loads = [
        pltpu.make_async_copy(src, dst, wsem.at[n])
        for n, (src, dst) in enumerate(((w_in, w1), (w_out, w2), (w_skip, w3)))
    ]
    x_load = pltpu.make_async_copy(lat, x, x_r.at[2])
    up_load = pltpu.make_async_copy(cot, up, up_r.at[2])

    @pl.when(s == 0)
    def _():
        x_load.start()

    for load in loads:
        load.start()

    @pl.when(s == 3)
    def _():
        up_load.start()

    barrier = pltpu.get_barrier_semaphore()
    for by in (1, 2, 3):
        pl.semaphore_signal(barrier, inc=1, device_id={"segment": (s + by) % 4}, device_id_type=MESH)
    for other in (along(0, 1), along(0, -1), along(1, 1), along(1, -1), partner):
        pl.semaphore_signal(barrier, inc=1, device_id={"dp": other}, device_id_type=MESH)
    row = lax.broadcasted_iota(jnp.int32, (8, table.shape[0]), 0)
    chosen = jnp.where(row == 0, steps[0, 0], steps[1, 0])
    hot = lax.broadcasted_iota(jnp.int32, (8, table.shape[0]), 1) == chosen
    found = jnp.dot(hot.astype(F32).astype(BF16), table[...], preferred_element_type=F32)
    bias[0] = found[0:1]
    bias[1] = found[1:2]
    pl.semaphore_wait(barrier, 8)

    def hand(buf, dst, m, send, recv, to):
        rows = pl.ds(pl.multiple_of(m * R, R), R)
        return pltpu.make_async_remote_copy(
            src_ref=buf.at[rows], dst_ref=dst.at[rows], send_sem=send.at[m], recv_sem=recv.at[m],
            device_id={"segment": to}, device_id_type=MESH,
        )

    def send_x(m):
        return hand(po, x, m, x_s, x_r, (s + 1) % 4)

    def send_sk(m):
        return hand(sk, sk, m, sk_s, sk_r, 3 - s)

    def send_up(m):
        return hand(gi, up, m, up_s, up_r, (s + 3) % 4)

    def send_dk(m):
        return hand(dk, dk, m, dk_s, dk_r, 3 - s)

    columns = [pl.ds(n * TILE, TILE) for n in range(C // TILE)]
    on3 = s // 3

    def ring(stage, msg, block, src, dst, axis, by):
        n = block[0] * 4 + block[1]
        return pltpu.make_async_remote_copy(
            src_ref=src, dst_ref=dst, send_sem=rs_s.at[stage, msg, n], recv_sem=rs_r.at[stage, msg, n],
            device_id={"dp": along(axis, by)}, device_id_type=MESH,
        )

    def piece(block, pos):
        k, _, col, width, colour, _ = block
        cols = pl.ds(col, width)
        if colour == 0:
            return grads.at[k, pos % 4, :, :, cols]
        return grads.at[k, :, pos % 4, :, cols]

    def first(block, msg):
        k, _, col, width, colour, by = block
        cols = pl.ds(col, width)
        pos = (z, y)[colour]
        if msg == 0:
            return ring(0, 0, block, piece(block, pos + 2), r1.at[k, :, :, cols], colour, by)
        if msg == 1:
            return ring(0, 1, block, r1.at[k, :, :, cols], r2.at[k, :, :, cols], colour, by)
        return ring(0, 2, block, piece(block, pos - by + 4), r3.at[k, :, :, cols], colour, -by)

    def second(block, msg):
        k, _, col, width, colour, by = block
        cols = pl.ds(col, width)
        pos = (y, z)[colour]
        axis = 1 - colour
        if msg == 0:
            return ring(1, 0, block, s1.at[k, (pos + 2) % 4, :, cols], q1.at[k, :, cols], axis, by)
        if msg == 1:
            return ring(1, 1, block, q1.at[k, :, cols], q2.at[k, :, cols], axis, by)
        return ring(1, 2, block, s1.at[k, (pos - by + 4) % 4, :, cols], q3.at[k, :, cols], axis, -by)

    def product(k, right):
        @pl.loop(0, 4)
        def _(zp):
            left = lt[k, pl.ds(pl.multiple_of(zp * 320, 320), 320), :]
            for n in columns:
                acc = jnp.dot(left, right[:, n], preferred_element_type=F32).astype(BF16)
                for yp in range(4):
                    grads[k, zp, yp, :, n] = acc[yp * 80 : (yp + 1) * 80]

    def begin(k):
        for block in BLOCKS[4 * k : 4 * k + 4]:
            first(block, 0).start()
            first(block, 2).start()

    @pl.loop(0, 4)
    def _(i):
        kind = on3 * (i % 2) + (1 - on3) * (i // 2)
        m = on3 * (i // 2) + (1 - on3) * (i % 2)
        rows = pl.ds(pl.multiple_of(m * R, R), R)

        @pl.when(kind == 0)
        def _():
            @pl.when((s == 0) & (m == 0))
            def _():
                x_load.wait()

            @pl.when(s > 0)
            def _():
                send_x(m).wait_recv()

            @pl.when(i == 0)
            def _():
                loads[0].wait()

            for n in columns:
                pre[rows, n] = jnp.dot(x[rows, :], w1[:, n], preferred_element_type=F32)

            @pl.when(i == 0)
            def _():
                loads[1].wait()
                loads[2].wait()

            @pl.when(s >= 2)
            def _():
                send_sk(m).wait_recv()
                for n in columns:
                    pre[rows, n] += jnp.dot(sk[rows, :], w3[:, n], preferred_element_type=F32)

            for n in columns:
                v = pre[rows, n] + bias[m, :, n]
                g = 1.0 / (1.0 + jnp.exp(-v))
                gat[rows, n] = (v * g).astype(BF16)
                pre[rows, n] = g * (1.0 + v * (1.0 - g))
            for n in columns:
                po[rows, n] = (
                    x[rows, n].astype(F32)
                    + jnp.dot(gat[rows, :], w2[:, n], preferred_element_type=F32)
                ).astype(BF16)

            @pl.when(s < 3)
            def _():
                send_x(m).start()

            @pl.when(s < 2)
            def _():
                for n in columns:
                    sk[rows, n] = jnp.dot(
                        po[rows, :], w3[:, n], preferred_element_type=F32
                    ).astype(BF16)

                @pl.when(s == 1)
                def _():
                    send_sk(m).start()

                    @pl.when(m == 1)
                    def _():
                        for j in range(2):
                            send_x(j).wait_send()
                            send_sk(j).wait_send()
                        pl.semaphore_signal(turn, inc=1, device_id={"segment": 0}, device_id_type=MESH)

                @pl.when(s == 0)
                def _():
                    @pl.when(m == 1)
                    def _():
                        pl.semaphore_wait(turn, 1)

                    send_sk(m).start()

        @pl.when(kind == 1)
        def _():
            @pl.when((s == 3) & (m == 0))
            def _():
                up_load.wait()

            @pl.when(s == 0)
            def _():
                send_dk(m).wait_recv()

                @pl.when(m == 1)
                def _():
                    product(2, dk)
                    begin(2)

            @pl.when(s < 3)
            def _():
                send_up(m).wait_recv()

            @pl.when(s == 1)
            def _():
                send_dk(m).wait_recv()

            @pl.when(s < 2)
            def _():
                for n in columns:
                    tot[rows, n] = (
                        up[rows, n].astype(F32)
                        + lax.dot_general(dk[rows, :], w3[n, :], NT, preferred_element_type=F32)
                    ).astype(BF16)

            @pl.when(s >= 2)
            def _():
                tot[rows, :] = up[rows, :]

            for n in columns:
                dpre[rows, n] = (
                    lax.dot_general(tot[rows, :], w2[n, :], NT, preferred_element_type=F32)
                    * pre[rows, n]
                ).astype(BF16)

            @pl.when(s == 2)
            def _():
                for n in columns:
                    dk[rows, n] = lax.dot_general(
                        dpre[rows, :], w3[n, :], NT, preferred_element_type=F32
                    ).astype(BF16)
                send_dk(m).start()

            for n in columns:
                gi[rows, n] = (
                    tot[rows, n].astype(F32)
                    + lax.dot_general(dpre[rows, :], w1[n, :], NT, preferred_element_type=F32)
                ).astype(BF16)

            @pl.when(s > 0)
            def _():
                send_up(m).start()

            @pl.when(s == 3)
            def _():
                for n in columns:
                    dk[rows, n] = lax.dot_general(
                        dpre[rows, :], w3[n, :], NT, preferred_element_type=F32
                    ).astype(BF16)
                send_dk(m).start()

        @pl.when(kind == on3)
        def _():
            for n in columns:
                lt[0, n, rows] = x[rows, n].T
                lt[1, n, rows] = gat[rows, n].T

            @pl.when(s < 2)
            def _():
                for n in columns:
                    lt[2, n, rows] = po[rows, n].T

            @pl.when(s >= 2)
            def _():
                for n in columns:
                    lt[2, n, rows] = sk[rows, n].T

    @pl.when(s == 1)
    def _():
        product(2, dk)
        begin(2)

    @pl.when(s >= 2)
    def _():
        product(2, dpre)
        begin(2)

    product(1, tot)
    begin(1)
    product(0, dpre)
    begin(0)
    order = BLOCKS[::-1]
    for block in order:
        k, _, col, width, colour, by = block
        cols = pl.ds(col, width)
        first(block, 0).wait_recv()
        pos = (z, y)[colour] + by + 4
        r1[k, :, :, cols] = (
            r1[k, :, :, cols].astype(F32) + piece(block, pos)[...].astype(F32)
        ).astype(BF16)
        first(block, 1).start()
    for block in order:
        k, _, col, width, colour, by = block
        cols = pl.ds(col, width)
        first(block, 1).wait_recv()
        first(block, 2).wait_recv()
        s1[k, :, :, cols] = (
            piece(block, (z, y)[colour])[...].astype(F32)
            + r2[k, :, :, cols].astype(F32)
            + r3[k, :, :, cols].astype(F32)
        ).astype(BF16)
        second(block, 0).start()
        second(block, 2).start()
    for block in order:
        k, _, col, width, colour, by = block
        cols = pl.ds(col, width)
        second(block, 0).wait_recv()
        pos = ((y, z)[colour] + by + 4) % 4
        q1[k, :, cols] = (q1[k, :, cols].astype(F32) + s1[k, pos, :, cols].astype(F32)).astype(BF16)
        second(block, 1).start()

    def pair(k):
        return pltpu.make_async_remote_copy(
            src_ref=xs.at[k, 1 - xh], dst_ref=xr.at[k], send_sem=xh_s.at[k], recv_sem=xh_r.at[k],
            device_id={"dp": partner}, device_id_type=MESH,
        )

    for block in order:
        k, last, col, width, colour, by = block
        cols = pl.ds(col, width)
        second(block, 1).wait_recv()
        second(block, 2).wait_recv()
        part = (
            s1[k, (y, z)[colour], :, cols].astype(F32)
            + q2[k, :, cols].astype(F32)
            + q3[k, :, cols].astype(F32)
        )
        xs[k, 0, :, cols] = part[:40].astype(BF16)
        xs[k, 1, :, cols] = part[40:].astype(BF16)
        if last == 0:
            pair(k).start()
    for k in (2, 1, 0):
        pair(k).wait_recv()
        (g_in, g_out, g_skip)[k][...] = xs[k, xh].astype(F32) + xr[k].astype(F32)
    for block in order:
        for msg in range(3):
            first(block, msg).wait_send()
            second(block, msg).wait_send()
    for k in range(3):
        pair(k).wait_send()
    for m in range(2):

        @pl.when((s == 0) | (s == 2))
        def _():
            send_x(m).wait_send()

        @pl.when(s == 0)
        def _():
            send_sk(m).wait_send()

        @pl.when(s > 0)
        def _():
            send_up(m).wait_send()

        @pl.when(s >= 2)
        def _():
            send_dk(m).wait_send()


def deliver(*refs):
    sem = refs[-1]
    copies = [pltpu.make_async_copy(refs[n], refs[5 + n], sem.at[n]) for n in range(5)]
    for copy in copies:
        copy.start()
    for copy in copies:
        copy.wait()


def body(latents, cotangent, timesteps, time_table, w_in, w_out, w_skip):
    rows = 2 * R
    vmem = pl.BlockSpec(memory_space=pltpu.VMEM)
    hbm = pl.BlockSpec(memory_space=pltpu.HBM)
    act = pltpu.VMEM((rows, C), BF16)
    weight = pltpu.VMEM((C, C), BF16)
    quarter = pltpu.VMEM((3, 4, 80, C), BF16)
    sixteenth = pltpu.VMEM((3, 80, C), BF16)
    dma = pltpu.SemaphoreType.DMA
    out_act = jax.ShapeDtypeStruct((rows, C), BF16)
    out_grad = jax.ShapeDtypeStruct((40, C), F32)
    outs = (out_act, out_act, out_grad, out_grad, out_grad)
    results = pl.pallas_call(
        kernel,
        name="window",
        out_shape=outs,
        in_specs=[vmem, vmem, pl.BlockSpec(memory_space=pltpu.SMEM), vmem, hbm, hbm, hbm],
        out_specs=[vmem] * 5,
        scratch_shapes=[
            weight, weight, weight,
            pltpu.VMEM((2, 1, C), F32),
            act, act, act, act,
            pltpu.VMEM((rows, C), F32),
            act, act, act,
            pltpu.VMEM((3, C, rows), BF16),
            pltpu.VMEM((3, 4, 4, 80, C), BF16),
            quarter, quarter, quarter, quarter,
            sixteenth, sixteenth, sixteenth,
            pltpu.VMEM((3, 2, 40, C), BF16),
            pltpu.VMEM((3, 40, C), BF16),
            dma((3,)),
            pltpu.SemaphoreType.REGULAR,
            dma((2,)), dma((3,)),
            dma((2,)), dma((2,)),
            dma((2,)), dma((3,)),
            dma((2,)), dma((2,)),
            dma((2, 3, 12)), dma((2, 3, 12)),
            dma((3,)), dma((3,)),
        ],
        compiler_params=pltpu.CompilerParams(
            collective_id=0, has_side_effects=True, vmem_limit_bytes=50_000_000
        ),
    )(
        latents.reshape(rows, C), cotangent.reshape(rows, C), timesteps, time_table.reshape(1000, C),
        w_in.reshape(C, C), w_out.reshape(C, C), w_skip.reshape(C, C),
    )
    po, gi, g_in, g_out, g_skip = pl.pallas_call(
        deliver,
        name="deliver",
        out_shape=outs,
        in_specs=[vmem] * 5,
        out_specs=[hbm] * 5,
        scratch_shapes=[dma((5,))],
        compiler_params=pltpu.CompilerParams(vmem_limit_bytes=4_000_000),
    )(*results)
    return (
        po.reshape(1, 2, R, C),
        gi.reshape(1, 2, R, C),
        g_in[None],
        g_out[None],
        g_skip[None],
    )


def solution(mesh):
    in_specs = (
        P(None, "dp", None),
        P(None, "dp", None),
        P(None, "dp"),
        P("segment", None, None),
        P("segment", None, None),
        P("segment", None, None),
        P("segment", None, None),
    )
    out_specs = (
        P("segment", None, "dp", None),
        P("segment", None, "dp", None),
        P("segment", "dp", None),
        P("segment", "dp", None),
        P("segment", "dp", None),
    )
    return jax.shard_map(body, mesh=mesh, in_specs=in_specs, out_specs=out_specs, check_vma=False)
```

```python
import jax
import jax.numpy as jnp
from jax import lax
from jax.experimental import pallas as pl
from jax.experimental.pallas import tpu as pltpu
from jax.sharding import PartitionSpec as P

MESH = pl.DeviceIdType.MESH
F32 = jnp.float32
BF16 = jnp.bfloat16
C = 1280
R = 128
TILE = 256
NT = (((1,), (1,)), ((), ()))
BLOCKS = ((0, 0, 384, 0, 1), (1, 384, 256, 0, -1), (2, 640, 256, 1, 1), (3, 896, 384, 1, -1))
Q = C // 4


def kernel(
    lat, cot, steps, table, w_in, w_out, w_skip,
    po, gi, g_in, g_out, g_skip,
    w1, w2, w3, bias, x, up, sk, dk, pre, gat, tot, dpre, lt, grads, r1, r2, r3, s1, q1, q2, q3, xs, xr,
    left, stage, right, part, p1, p2, p3, hs, hr, fs, fr,
    wsem, turn, x_s, x_r, sk_s, sk_r, up_s, up_r, dk_s, dk_r, rs_s, rs_r, xh_s, xh_r,
    ag_s, ag_r, fw_s, fw_r, aa_s, aa_r, js_s, js_r, fin_s, fin_r,
):
    s = lax.axis_index("segment")
    dp = lax.axis_index("dp")
    z = dp // 8
    y = (dp // 2) % 4
    xh = dp % 2

    def along(axis, by):
        if axis == 0:
            return ((z + by + 4) % 4) * 8 + y * 2 + xh
        return z * 8 + ((y + by + 4) % 4) * 2 + xh

    partner = z * 8 + y * 2 + (1 - xh)
    loads = [
        pltpu.make_async_copy(src, dst, wsem.at[n])
        for n, (src, dst) in enumerate(((w_in, w1), (w_out, w2), (w_skip, w3)))
    ]
    x_load = pltpu.make_async_copy(lat, x, x_r.at[2])
    up_load = pltpu.make_async_copy(cot, up, up_r.at[2])

    @pl.when(s == 0)
    def _():
        x_load.start()

    for load in loads:
        load.start()

    @pl.when(s == 3)
    def _():
        up_load.start()

    barrier = pltpu.get_barrier_semaphore()
    for by in (1, 2, 3):
        pl.semaphore_signal(barrier, inc=1, device_id={"segment": (s + by) % 4}, device_id_type=MESH)
    for other in [along(axis, by) for axis in (0, 1) for by in (1, 2, 3)] + [partner]:
        pl.semaphore_signal(barrier, inc=1, device_id={"dp": other}, device_id_type=MESH)
    row = lax.broadcasted_iota(jnp.int32, (8, table.shape[0]), 0)
    chosen = jnp.where(row == 0, steps[0, 0], steps[1, 0])
    hot = lax.broadcasted_iota(jnp.int32, (8, table.shape[0]), 1) == chosen
    found = jnp.dot(hot.astype(F32).astype(BF16), table[...], preferred_element_type=F32)
    bias[0] = found[0:1]
    bias[1] = found[1:2]
    pl.semaphore_wait(barrier, 10)

    def hand(buf, dst, m, send, recv, to):
        rows = pl.ds(pl.multiple_of(m * R, R), R)
        return pltpu.make_async_remote_copy(
            src_ref=buf.at[rows], dst_ref=dst.at[rows], send_sem=send.at[m], recv_sem=recv.at[m],
            device_id={"segment": to}, device_id_type=MESH,
        )

    def send_x(m):
        return hand(po, x, m, x_s, x_r, (s + 1) % 4)

    def send_sk(m):
        return hand(sk, sk, m, sk_s, sk_r, 3 - s)

    def send_up(m):
        return hand(gi, up, m, up_s, up_r, (s + 3) % 4)

    def send_dk(m):
        return hand(dk, dk, m, dk_s, dk_r, 3 - s)

    columns = [pl.ds(n * TILE, TILE) for n in range(C // TILE)]
    on3 = s // 3

    here = (z, y)

    def ring(step, msg, block, src, dst, axis, by):
        n = block[0]
        return pltpu.make_async_remote_copy(
            src_ref=src, dst_ref=dst, send_sem=rs_s.at[step, msg, n], recv_sem=rs_r.at[step, msg, n],
            device_id={"dp": along(axis, by)}, device_id_type=MESH,
        )

    def piece(block, pos):
        _, col, width, colour, _ = block
        cols = pl.ds(col, width)
        if colour == 0:
            return grads.at[pos % 4, :, :, cols]
        return grads.at[:, pos % 4, :, cols]

    def first(block, msg):
        _, col, width, colour, by = block
        cols = pl.ds(col, width)
        pos = here[colour]
        if msg == 0:
            return ring(0, 0, block, piece(block, pos + 2), r1.at[:, :, cols], colour, by)
        if msg == 1:
            return ring(0, 1, block, r1.at[:, :, cols], r2.at[:, :, cols], colour, by)
        return ring(0, 2, block, piece(block, pos - by + 4), r3.at[:, :, cols], colour, -by)

    def second(block, msg):
        _, col, width, colour, by = block
        cols = pl.ds(col, width)
        axis = 1 - colour
        pos = here[axis]
        if msg == 0:
            return ring(1, 0, block, s1.at[(pos + 2) % 4, :, cols], q1.at[:, cols], axis, by)
        if msg == 1:
            return ring(1, 1, block, q1.at[:, cols], q2.at[:, cols], axis, by)
        return ring(1, 2, block, s1.at[(pos - by + 4) % 4, :, cols], q3.at[:, cols], axis, -by)

    def product(other):
        @pl.loop(0, 4)
        def _(zp):
            mine = lt[pl.ds(pl.multiple_of(zp * 320, 320), 320), :]
            for n in columns:
                acc = jnp.dot(mine, other[:, n], preferred_element_type=F32).astype(BF16)
                for yp in range(4):
                    grads[zp, yp, :, n] = acc[yp * 80 : (yp + 1) * 80]

        for block in BLOCKS:
            first(block, 0).start()
            first(block, 2).start()

    def remote(src, dst, send, recv, axis, by):
        return pltpu.make_async_remote_copy(
            src_ref=src, dst_ref=dst, send_sem=send, recv_sem=recv,
            device_id={"dp": along(axis, by)}, device_id_type=MESH,
        )

    def slot(job, m, by=0):
        return pl.ds(pl.multiple_of(((here[job] + by + 4) % 4 * 2 + m) * R, R), R)

    def spread(job, m, d):
        ref = left.at[job, :, slot(job, m)]
        return remote(ref, ref, ag_s.at[job, m, d], ag_r.at[job, m, d], job, 1 - 2 * d)

    def relay(job, m, d):
        by = 1 - 2 * d
        ref = left.at[job, pl.ds(d * 640, 640), slot(job, m, -by)]
        return remote(ref, ref, fw_s.at[job, m, d], fw_r.at[job, m, d], job, by)

    def forward(m):
        for job in range(2):
            for d in range(2):
                spread(job, m, d).wait_recv()
                relay(job, m, d).start()

    def turned(job, m, by):
        rows = pl.ds(pl.multiple_of(m * R, R), R)
        return remote(
            stage.at[job, (here[job] + by) % 4, rows], right.at[job, slot(job, m)],
            aa_s.at[job, m, by - 1], aa_r.at[job, m, by - 1], job, by,
        )

    def swap(job, m):
        rows = pl.ds(pl.multiple_of(m * R, R), R)
        value = (dpre, tot)[job]
        for q in range(4):
            stage[job, q, rows, :] = value[rows, q * Q : (q + 1) * Q]
        for by in (1, 3, 2):
            turned(job, m, by).start()
        right[job, slot(job, m), :] = stage[job, here[job], rows, :]

    def sums(job, half, msg):
        by = 1 - 2 * half
        axis = 1 - job
        pos = here[axis]
        o = pl.ds(2 * half, 2)
        sems = (js_s.at[job, half, msg], js_r.at[job, half, msg])
        if msg == 0:
            return remote(part.at[job, o, (pos + 2) % 4], p1.at[job, o], *sems, axis, by)
        if msg == 1:
            return remote(p1.at[job, o], p2.at[job, o], *sems, axis, by)
        return remote(part.at[job, o, (pos - by + 4) % 4], p3.at[job, o], *sems, axis, -by)

    def block_product(job):
        @pl.loop(0, 4)
        def _(zp):
            acc = jnp.dot(
                left[job, pl.ds(pl.multiple_of(zp * 320, 320), 320), :], right[job],
                preferred_element_type=F32,
            ).astype(BF16)
            for yp in range(4):
                if job == 0:
                    part[0, zp, yp] = acc[yp * 80 : (yp + 1) * 80]
                else:
                    part[1, yp, zp] = acc[yp * 80 : (yp + 1) * 80]

        for half in range(2):
            sums(job, half, 0).start()
            sums(job, half, 2).start()

    def pair(k):
        src, dst = ((hs.at[0, 1 - xh], hr.at[0]), (hs.at[1, 1 - xh], hr.at[1]), (xs.at[1 - xh], xr))[k]
        return pltpu.make_async_remote_copy(
            src_ref=src, dst_ref=dst, send_sem=xh_s.at[k], recv_sem=xh_r.at[k],
            device_id={"dp": partner}, device_id_type=MESH,
        )

    def last(job, by):
        return remote(
            fs.at[job, (here[job] + by) % 4], fr.at[job, here[job]],
            fin_s.at[job, by - 1], fin_r.at[job, by - 1], job, by,
        )

    @pl.loop(0, 4)
    def _(i):
        kind = on3 * (i % 2) + (1 - on3) * (i // 2)
        m = on3 * (i // 2) + (1 - on3) * (i % 2)
        rows = pl.ds(pl.multiple_of(m * R, R), R)

        @pl.when(kind == 0)
        def _():
            @pl.when((s == 0) & (m == 0))
            def _():
                x_load.wait()

            @pl.when(s > 0)
            def _():
                send_x(m).wait_recv()

            @pl.when(i == 0)
            def _():
                loads[0].wait()

            for n in columns:
                pre[rows, n] = jnp.dot(x[rows, :], w1[:, n], preferred_element_type=F32)

            @pl.when(i == 0)
            def _():
                loads[1].wait()
                loads[2].wait()

            @pl.when(s >= 2)
            def _():
                send_sk(m).wait_recv()
                for n in columns:
                    pre[rows, n] += jnp.dot(sk[rows, :], w3[:, n], preferred_element_type=F32)

            for n in columns:
                v = pre[rows, n] + bias[m, :, n]
                g = 1.0 / (1.0 + jnp.exp(-v))
                gat[rows, n] = (v * g).astype(BF16)
                pre[rows, n] = g * (1.0 + v * (1.0 - g))
            for n in columns:
                po[rows, n] = (
                    x[rows, n].astype(F32)
                    + jnp.dot(gat[rows, :], w2[:, n], preferred_element_type=F32)
                ).astype(BF16)

            @pl.when(s < 3)
            def _():
                send_x(m).start()

            @pl.when(s < 2)
            def _():
                for n in columns:
                    sk[rows, n] = jnp.dot(
                        po[rows, :], w3[:, n], preferred_element_type=F32
                    ).astype(BF16)

                @pl.when(s == 1)
                def _():
                    send_sk(m).start()

                    @pl.when(m == 1)
                    def _():
                        for j in range(2):
                            send_x(j).wait_send()
                            send_sk(j).wait_send()
                        pl.semaphore_signal(turn, inc=1, device_id={"segment": 0}, device_id_type=MESH)

                @pl.when(s == 0)
                def _():
                    @pl.when(m == 1)
                    def _():
                        pl.semaphore_wait(turn, 1)

                    send_sk(m).start()

        @pl.when(kind == 1)
        def _():
            @pl.when((s == 3) & (m == 0))
            def _():
                up_load.wait()

            @pl.when(s == 0)
            def _():
                send_dk(m).wait_recv()

                @pl.when(m == 1)
                def _():
                    product(dk)

            @pl.when(s < 3)
            def _():
                send_up(m).wait_recv()

            @pl.when(s == 1)
            def _():
                send_dk(m).wait_recv()

            @pl.when(s < 2)
            def _():
                for n in columns:
                    tot[rows, n] = (
                        up[rows, n].astype(F32)
                        + lax.dot_general(dk[rows, :], w3[n, :], NT, preferred_element_type=F32)
                    ).astype(BF16)

            @pl.when(s >= 2)
            def _():
                tot[rows, :] = up[rows, :]

            for n in columns:
                dpre[rows, n] = (
                    lax.dot_general(tot[rows, :], w2[n, :], NT, preferred_element_type=F32)
                    * pre[rows, n]
                ).astype(BF16)

            @pl.when(s == 0)
            def _():
                swap(1, m)
                swap(0, m)

            @pl.when(s == 2)
            def _():
                for n in columns:
                    dk[rows, n] = lax.dot_general(
                        dpre[rows, :], w3[n, :], NT, preferred_element_type=F32
                    ).astype(BF16)
                send_dk(m).start()

            for n in columns:
                gi[rows, n] = (
                    tot[rows, n].astype(F32)
                    + lax.dot_general(dpre[rows, :], w1[n, :], NT, preferred_element_type=F32)
                ).astype(BF16)

            @pl.when(s > 0)
            def _():
                send_up(m).start()

            @pl.when(s == 3)
            def _():
                for n in columns:
                    dk[rows, n] = lax.dot_general(
                        dpre[rows, :], w3[n, :], NT, preferred_element_type=F32
                    ).astype(BF16)
                send_dk(m).start()

            @pl.when(s > 0)
            def _():
                swap(1, m)
                swap(0, m)

        @pl.when(kind == on3)
        def _():
            for n in columns:
                left[0, n, slot(0, m)] = x[rows, n].T
                left[1, n, slot(1, m)] = gat[rows, n].T
            for job in range(2):
                for d in range(2):
                    spread(job, m, d).start()

            @pl.when(s < 2)
            def _():
                for n in columns:
                    lt[n, rows] = po[rows, n].T

            @pl.when(s >= 2)
            def _():
                for n in columns:
                    lt[n, rows] = sk[rows, n].T

        @pl.when((i >= 1 + 2 * on3) & (i <= 2 + on3))
        def _():
            forward(i - 1 - 2 * on3)

    @pl.when(s == 3)
    def _():
        forward(1)

    @pl.when(s == 1)
    def _():
        product(dk)

    @pl.when(s >= 2)
    def _():
        product(dpre)

    def gathered(job):
        for m in range(2):
            for d in range(2):
                relay(job, m, d).wait_recv()
            for by in (1, 2, 3):
                turned(job, m, by).wait_recv()

    gathered(1)
    block_product(1)
    for block in BLOCKS:
        _, col, width, colour, by = block
        cols = pl.ds(col, width)
        first(block, 0).wait_recv()
        r1[:, :, cols] = (
            r1[:, :, cols].astype(F32) + piece(block, here[colour] + by + 4)[...].astype(F32)
        ).astype(BF16)
        first(block, 1).start()
    gathered(0)
    block_product(0)
    for job in (1, 0):
        for half in range(2):
            o = pl.ds(2 * half, 2)
            sums(job, half, 0).wait_recv()
            pos = (here[1 - job] + 5 - 2 * half) % 4
            p1[job, o] = (p1[job, o].astype(F32) + part[job, o, pos].astype(F32)).astype(BF16)
            sums(job, half, 1).start()
    for block in BLOCKS:
        _, col, width, colour, by = block
        cols = pl.ds(col, width)
        first(block, 1).wait_recv()
        first(block, 2).wait_recv()
        s1[:, :, cols] = (
            piece(block, here[colour])[...].astype(F32)
            + r2[:, :, cols].astype(F32)
            + r3[:, :, cols].astype(F32)
        ).astype(BF16)
        second(block, 0).start()
        second(block, 2).start()
    for job in (1, 0):
        for half in range(2):
            sums(job, half, 1).wait_recv()
            sums(job, half, 2).wait_recv()
            for o in (2 * half, 2 * half + 1):
                total = (
                    part[job, o, here[1 - job]].astype(F32)
                    + p2[job, o].astype(F32)
                    + p3[job, o].astype(F32)
                )
                hs[job, 0, o] = total[:40].astype(BF16)
                hs[job, 1, o] = total[40:].astype(BF16)
        pair(job).start()
    for block in BLOCKS:
        _, col, width, colour, by = block
        cols = pl.ds(col, width)
        second(block, 0).wait_recv()
        pos = (here[1 - colour] + by + 4) % 4
        q1[:, cols] = (q1[:, cols].astype(F32) + s1[pos, :, cols].astype(F32)).astype(BF16)
        second(block, 1).start()
    for job in (1, 0):
        pair(job).wait_recv()
        for o in range(4):
            fs[job, o] = (hs[job, xh, o].astype(F32) + hr[job, o].astype(F32)).astype(BF16)
        for by in (1, 3, 2):
            last(job, by).start()
        fr[job, here[job]] = fs[job, here[job]]
    for block in BLOCKS:
        _, col, width, colour, by = block
        cols = pl.ds(col, width)
        second(block, 1).wait_recv()
        second(block, 2).wait_recv()
        total = (
            s1[here[1 - colour], :, cols].astype(F32)
            + q2[:, cols].astype(F32)
            + q3[:, cols].astype(F32)
        )
        xs[0, :, cols] = total[:40].astype(BF16)
        xs[1, :, cols] = total[40:].astype(BF16)
    pair(2).start()
    for job in (1, 0):
        for by in (1, 2, 3):
            last(job, by).wait_recv()
        for q in range(4):
            (g_in, g_out)[job][:, q * Q : (q + 1) * Q] = fr[job, q].astype(F32)
    pair(2).wait_recv()
    g_skip[...] = xs[xh].astype(F32) + xr[...].astype(F32)
    for block in BLOCKS:
        for msg in range(3):
            first(block, msg).wait_send()
            second(block, msg).wait_send()
    for k in range(3):
        pair(k).wait_send()
    for job in range(2):
        for n in range(3):
            last(job, n + 1).wait_send()
            for m in range(2):
                turned(job, m, n + 1).wait_send()
                sums(job, m, n).wait_send()
        for m in range(2):
            for d in range(2):
                spread(job, m, d).wait_send()
                relay(job, m, d).wait_send()
    for m in range(2):

        @pl.when((s == 0) | (s == 2))
        def _():
            send_x(m).wait_send()

        @pl.when(s == 0)
        def _():
            send_sk(m).wait_send()

        @pl.when(s > 0)
        def _():
            send_up(m).wait_send()

        @pl.when(s >= 2)
        def _():
            send_dk(m).wait_send()


def deliver(*refs):
    sem = refs[-1]
    copies = [pltpu.make_async_copy(refs[n], refs[5 + n], sem.at[n]) for n in range(5)]
    for copy in copies:
        copy.start()
    for copy in copies:
        copy.wait()


def body(latents, cotangent, timesteps, time_table, w_in, w_out, w_skip):
    rows = 2 * R
    vmem = pl.BlockSpec(memory_space=pltpu.VMEM)
    hbm = pl.BlockSpec(memory_space=pltpu.HBM)
    act = pltpu.VMEM((rows, C), BF16)
    weight = pltpu.VMEM((C, C), BF16)
    quarter = pltpu.VMEM((4, 80, C), BF16)
    sixteenth = pltpu.VMEM((80, C), BF16)
    sums = pltpu.VMEM((2, 4, 80, Q), BF16)
    halves = pltpu.VMEM((2, 4, 40, Q), BF16)
    dma = pltpu.SemaphoreType.DMA
    out_act = jax.ShapeDtypeStruct((rows, C), BF16)
    out_grad = jax.ShapeDtypeStruct((40, C), F32)
    outs = (out_act, out_act, out_grad, out_grad, out_grad)
    results = pl.pallas_call(
        kernel,
        name="window",
        out_shape=outs,
        in_specs=[vmem, vmem, pl.BlockSpec(memory_space=pltpu.SMEM), vmem, hbm, hbm, hbm],
        out_specs=[vmem] * 5,
        scratch_shapes=[
            weight, weight, weight,
            pltpu.VMEM((2, 1, C), F32),
            act, act, act, act,
            pltpu.VMEM((rows, C), F32),
            act, act, act,
            pltpu.VMEM((C, rows), BF16),
            pltpu.VMEM((4, 4, 80, C), BF16),
            quarter, quarter, quarter, quarter,
            sixteenth, sixteenth, sixteenth,
            pltpu.VMEM((2, 40, C), BF16),
            pltpu.VMEM((40, C), BF16),
            pltpu.VMEM((2, C, 4 * rows), BF16),
            pltpu.VMEM((2, 4, rows, Q), BF16),
            pltpu.VMEM((2, 4 * rows, Q), BF16),
            pltpu.VMEM((2, 4, 4, 80, Q), BF16),
            sums, sums, sums,
            pltpu.VMEM((2, 2, 4, 40, Q), BF16),
            halves, halves, halves,
            dma((3,)),
            pltpu.SemaphoreType.REGULAR,
            dma((2,)), dma((3,)),
            dma((2,)), dma((2,)),
            dma((2,)), dma((3,)),
            dma((2,)), dma((2,)),
            dma((2, 3, 4)), dma((2, 3, 4)),
            dma((3,)), dma((3,)),
            dma((2, 2, 2)), dma((2, 2, 2)),
            dma((2, 2, 2)), dma((2, 2, 2)),
            dma((2, 2, 3)), dma((2, 2, 3)),
            dma((2, 2, 3)), dma((2, 2, 3)),
            dma((2, 3)), dma((2, 3)),
        ],
        compiler_params=pltpu.CompilerParams(
            collective_id=0, has_side_effects=True, vmem_limit_bytes=50_000_000
        ),
    )(
        latents.reshape(rows, C), cotangent.reshape(rows, C), timesteps, time_table.reshape(1000, C),
        w_in.reshape(C, C), w_out.reshape(C, C), w_skip.reshape(C, C),
    )
    po, gi, g_in, g_out, g_skip = pl.pallas_call(
        deliver,
        name="deliver",
        out_shape=outs,
        in_specs=[vmem] * 5,
        out_specs=[hbm] * 5,
        scratch_shapes=[dma((5,))],
        compiler_params=pltpu.CompilerParams(vmem_limit_bytes=4_000_000),
    )(*results)
    return (
        po.reshape(1, 2, R, C),
        gi.reshape(1, 2, R, C),
        g_in[None],
        g_out[None],
        g_skip[None],
    )


def solution(mesh):
    in_specs = (
        P(None, "dp", None),
        P(None, "dp", None),
        P(None, "dp"),
        P("segment", None, None),
        P("segment", None, None),
        P("segment", None, None),
        P("segment", None, None),
    )
    out_specs = (
        P("segment", None, "dp", None),
        P("segment", None, "dp", None),
        P("segment", "dp", None),
        P("segment", "dp", None),
        P("segment", "dp", None),
    )
    return jax.shard_map(body, mesh=mesh, in_specs=in_specs, out_specs=out_specs, check_vma=False)
```

```python
import jax
import jax.numpy as jnp
from jax import lax
from jax.experimental import pallas as pl
from jax.experimental.pallas import tpu as pltpu
from jax.sharding import PartitionSpec as P

MESH = pl.DeviceIdType.MESH
F32 = jnp.float32
BF16 = jnp.bfloat16
C = 1280
R = 128
TILE = 256
NT = (((1,), (1,)), ((), ()))
BLOCKS = ((0, 0, 384, 0, 1), (1, 384, 256, 0, -1), (2, 640, 256, 1, 1), (3, 896, 384, 1, -1))
Q = C // 4


def kernel(
    lat, cot, steps, table, w_in, w_out, w_skip,
    po, gi, g_in, g_out, g_skip,
    w1, w2, w3, rows_t, bias, acc, x, up, sk, dk, pre, gat, tot, dpre, lt, grads, r1, r2, r3, s1, q1, q2, q3, xs, xr,
    left, stage, right, part, p1, p2, p3, hs, hr, fs, fr,
    wsem, turn, x_s, x_r, sk_s, sk_r, up_s, up_r, dk_s, dk_r, rs_s, rs_r, xh_s, xh_r,
    ag_s, ag_r, fw_s, fw_r, aa_s, aa_r, js_s, js_r, fin_s, fin_r,
):
    s = lax.axis_index("segment")
    dp = lax.axis_index("dp")
    z = dp // 8
    y = (dp // 2) % 4
    xh = dp % 2

    def along(axis, by):
        if axis == 0:
            return ((z + by + 4) % 4) * 8 + y * 2 + xh
        return z * 8 + ((y + by + 4) % 4) * 2 + xh

    partner = z * 8 + y * 2 + (1 - xh)
    loads = [
        pltpu.make_async_copy(src, dst, wsem.at[n])
        for n, (src, dst) in enumerate(((w_in, w1), (table, rows_t), (w_out, w2), (w_skip, w3)))
    ]
    x_load = pltpu.make_async_copy(lat, x, x_r.at[2])
    up_load = pltpu.make_async_copy(cot, up, up_r.at[2])

    @pl.when(s == 0)
    def _():
        x_load.start()

    for load in loads:
        load.start()

    @pl.when(s == 3)
    def _():
        up_load.start()

    barrier = pltpu.get_barrier_semaphore()
    for by in (1, 2, 3):
        pl.semaphore_signal(barrier, inc=1, device_id={"segment": (s + by) % 4}, device_id_type=MESH)
    for other in [along(axis, by) for axis in (0, 1) for by in (1, 2, 3)] + [partner]:
        pl.semaphore_signal(barrier, inc=1, device_id={"dp": other}, device_id_type=MESH)

    def hand(buf, dst, m, send, recv, to):
        rows = pl.ds(pl.multiple_of(m * R, R), R)
        return pltpu.make_async_remote_copy(
            src_ref=buf.at[rows], dst_ref=dst.at[rows], send_sem=send.at[m], recv_sem=recv.at[m],
            device_id={"segment": to}, device_id_type=MESH,
        )

    def send_x(m):
        return hand(po, x, m, x_s, x_r, (s + 1) % 4)

    def send_sk(m):
        return hand(sk, sk, m, sk_s, sk_r, 3 - s)

    def send_up(m):
        return hand(gi, up, m, up_s, up_r, (s + 3) % 4)

    def send_dk(m):
        return hand(dk, dk, m, dk_s, dk_r, 3 - s)

    columns = [pl.ds(n * TILE, TILE) for n in range(C // TILE)]
    on3 = s // 3

    here = (z, y)

    def ring(step, msg, block, src, dst, axis, by):
        n = block[0]
        return pltpu.make_async_remote_copy(
            src_ref=src, dst_ref=dst, send_sem=rs_s.at[step, msg, n], recv_sem=rs_r.at[step, msg, n],
            device_id={"dp": along(axis, by)}, device_id_type=MESH,
        )

    def piece(block, pos):
        _, col, width, colour, _ = block
        cols = pl.ds(col, width)
        if colour == 0:
            return grads.at[pos % 4, :, :, cols]
        return grads.at[:, pos % 4, :, cols]

    def first(block, msg):
        _, col, width, colour, by = block
        cols = pl.ds(col, width)
        pos = here[colour]
        if msg == 0:
            return ring(0, 0, block, piece(block, pos + 2), r1.at[:, :, cols], colour, by)
        if msg == 1:
            return ring(0, 1, block, r1.at[:, :, cols], r2.at[:, :, cols], colour, by)
        return ring(0, 2, block, piece(block, pos - by + 4), r3.at[:, :, cols], colour, -by)

    def second(block, msg):
        _, col, width, colour, by = block
        cols = pl.ds(col, width)
        axis = 1 - colour
        pos = here[axis]
        if msg == 0:
            return ring(1, 0, block, s1.at[(pos + 2) % 4, :, cols], q1.at[:, cols], axis, by)
        if msg == 1:
            return ring(1, 1, block, q1.at[:, cols], q2.at[:, cols], axis, by)
        return ring(1, 2, block, s1.at[(pos - by + 4) % 4, :, cols], q3.at[:, cols], axis, -by)

    def product(other):
        @pl.loop(0, 4)
        def _(zp):
            mine = lt[pl.ds(pl.multiple_of(zp * 320, 320), 320), :]
            for n in columns:
                acc = jnp.dot(mine, other[:, n], preferred_element_type=F32).astype(BF16)
                for yp in range(4):
                    grads[zp, yp, :, n] = acc[yp * 80 : (yp + 1) * 80]

        for block in BLOCKS:
            first(block, 0).start()
            first(block, 2).start()

    def remote(src, dst, send, recv, axis, by):
        return pltpu.make_async_remote_copy(
            src_ref=src, dst_ref=dst, send_sem=send, recv_sem=recv,
            device_id={"dp": along(axis, by)}, device_id_type=MESH,
        )

    def slot(job, m, by=0):
        return pl.ds(pl.multiple_of(((here[job] + by + 4) % 4 * 2 + m) * R, R), R)

    def spread(job, m, d):
        ref = left.at[job, :, slot(job, m)]
        return remote(ref, ref, ag_s.at[job, m, d], ag_r.at[job, m, d], job, 1 - 2 * d)

    def relay(job, m, d):
        by = 1 - 2 * d
        ref = left.at[job, pl.ds(d * 640, 640), slot(job, m, -by)]
        return remote(ref, ref, fw_s.at[job, m, d], fw_r.at[job, m, d], job, by)

    def forward(m):
        for job in range(2):
            for d in range(2):
                spread(job, m, d).wait_recv()
                relay(job, m, d).start()

    def turned(job, m, by):
        rows = pl.ds(pl.multiple_of(m * R, R), R)
        return remote(
            stage.at[job, (here[job] + by) % 4, rows], right.at[job, slot(job, m)],
            aa_s.at[job, m, by - 1], aa_r.at[job, m, by - 1], job, by,
        )

    def swap(job, m):
        rows = pl.ds(pl.multiple_of(m * R, R), R)
        value = (dpre, tot)[job]
        for q in range(4):
            stage[job, q, rows, :] = value[rows, q * Q : (q + 1) * Q]
        for by in (1, 3, 2):
            turned(job, m, by).start()
        right[job, slot(job, m), :] = stage[job, here[job], rows, :]

    def sums(job, half, msg):
        by = 1 - 2 * half
        axis = 1 - job
        pos = here[axis]
        o = pl.ds(2 * half, 2)
        sems = (js_s.at[job, half, msg], js_r.at[job, half, msg])
        if msg == 0:
            return remote(part.at[job, o, (pos + 2) % 4], p1.at[job, o], *sems, axis, by)
        if msg == 1:
            return remote(p1.at[job, o], p2.at[job, o], *sems, axis, by)
        return remote(part.at[job, o, (pos - by + 4) % 4], p3.at[job, o], *sems, axis, -by)

    def block_product(job):
        @pl.loop(0, 4)
        def _(zp):
            acc = jnp.dot(
                left[job, pl.ds(pl.multiple_of(zp * 320, 320), 320), :], right[job],
                preferred_element_type=F32,
            ).astype(BF16)
            for yp in range(4):
                if job == 0:
                    part[0, zp, yp] = acc[yp * 80 : (yp + 1) * 80]
                else:
                    part[1, yp, zp] = acc[yp * 80 : (yp + 1) * 80]

        for half in range(2):
            sums(job, half, 0).start()
            sums(job, half, 2).start()

    def pair(k):
        src, dst = ((hs.at[0, 1 - xh], hr.at[0]), (hs.at[1, 1 - xh], hr.at[1]), (xs.at[1 - xh], xr))[k]
        return pltpu.make_async_remote_copy(
            src_ref=src, dst_ref=dst, send_sem=xh_s.at[k], recv_sem=xh_r.at[k],
            device_id={"dp": partner}, device_id_type=MESH,
        )

    def last(job, by):
        return remote(
            fs.at[job, (here[job] + by) % 4], fr.at[job, here[job]],
            fin_s.at[job, by - 1], fin_r.at[job, by - 1], job, by,
        )

    @pl.loop(0, 4)
    def _(i):
        kind = on3 * (i % 2) + (1 - on3) * (i // 2)
        m = on3 * (i // 2) + (1 - on3) * (i % 2)
        rows = pl.ds(pl.multiple_of(m * R, R), R)

        @pl.when(kind == 0)
        def _():
            @pl.when((s == 0) & (m == 0))
            def _():
                x_load.wait()

            @pl.when(s > 0)
            def _():
                send_x(m).wait_recv()

            @pl.when(i == 0)
            def _():
                loads[0].wait()

            for n in columns:
                pre[rows, n] = jnp.dot(x[rows, :], w1[:, n], preferred_element_type=F32)

            @pl.when(i == 0)
            def _():
                loads[1].wait()
                row = lax.broadcasted_iota(jnp.int32, (8, table.shape[0]), 0)
                chosen = jnp.where(row == 0, steps[0], steps[1])
                hot = lax.broadcasted_iota(jnp.int32, (8, table.shape[0]), 1) == chosen
                found = jnp.dot(hot.astype(F32).astype(BF16), rows_t[...], preferred_element_type=F32)
                bias[0] = found[0:1]
                bias[1] = found[1:2]
                loads[2].wait()
                loads[3].wait()

            @pl.when(s >= 2)
            def _():
                send_sk(m).wait_recv()
                for n in columns:
                    pre[rows, n] += jnp.dot(sk[rows, :], w3[:, n], preferred_element_type=F32)

            for n in columns:
                v = pre[rows, n] + bias[m, :, n]
                g = 1.0 / (1.0 + jnp.exp(-v))
                gat[rows, n] = (v * g).astype(BF16)
                pre[rows, n] = g * (1.0 + v * (1.0 - g))
            for n in columns:
                po[rows, n] = (
                    x[rows, n].astype(F32)
                    + jnp.dot(gat[rows, :], w2[:, n], preferred_element_type=F32)
                ).astype(BF16)

            @pl.when(i == 0)
            def _():
                pl.semaphore_wait(barrier, 10)

            @pl.when(s < 3)
            def _():
                send_x(m).start()

            @pl.when(s < 2)
            def _():
                for n in columns:
                    sk[rows, n] = jnp.dot(
                        po[rows, :], w3[:, n], preferred_element_type=F32
                    ).astype(BF16)

                @pl.when(s == 1)
                def _():
                    send_sk(m).start()

                    @pl.when(m == 1)
                    def _():
                        for j in range(2):
                            send_x(j).wait_send()
                            send_sk(j).wait_send()
                        pl.semaphore_signal(turn, inc=1, device_id={"segment": 0}, device_id_type=MESH)

                @pl.when(s == 0)
                def _():
                    @pl.when(m == 1)
                    def _():
                        pl.semaphore_wait(turn, 1)

                    send_sk(m).start()

        @pl.when(kind == 1)
        def _():
            @pl.when((s == 3) & (m == 0))
            def _():
                up_load.wait()

            @pl.when(s < 2)
            def _():
                send_dk(m).wait_recv()
                for n in columns:
                    acc[:, n] = lax.dot_general(
                        dk[rows, :], w3[n, :], NT, preferred_element_type=F32
                    )

                @pl.when(m == 1)
                def _():
                    product(dk)

            @pl.when(s < 3)
            def _():
                send_up(m).wait_recv()

            @pl.when(s < 2)
            def _():
                tot[rows, :] = (up[rows, :].astype(F32) + acc[...]).astype(BF16)

            @pl.when(s >= 2)
            def _():
                tot[rows, :] = up[rows, :]

            for n in columns:
                dpre[rows, n] = (
                    lax.dot_general(tot[rows, :], w2[n, :], NT, preferred_element_type=F32)
                    * pre[rows, n]
                ).astype(BF16)

            @pl.when(s == 0)
            def _():
                swap(1, m)
                swap(0, m)

            @pl.when(s == 2)
            def _():
                for n in columns:
                    dk[rows, n] = lax.dot_general(
                        dpre[rows, :], w3[n, :], NT, preferred_element_type=F32
                    ).astype(BF16)
                send_dk(m).start()

            for n in columns:
                gi[rows, n] = (
                    tot[rows, n].astype(F32)
                    + lax.dot_general(dpre[rows, :], w1[n, :], NT, preferred_element_type=F32)
                ).astype(BF16)

            @pl.when(s > 0)
            def _():
                send_up(m).start()

            @pl.when(s == 3)
            def _():
                for n in columns:
                    dk[rows, n] = lax.dot_general(
                        dpre[rows, :], w3[n, :], NT, preferred_element_type=F32
                    ).astype(BF16)
                send_dk(m).start()

            @pl.when(s > 0)
            def _():
                swap(1, m)
                swap(0, m)

        @pl.when(kind == on3)
        def _():
            for n in columns:
                left[0, n, slot(0, m)] = x[rows, n].T
                left[1, n, slot(1, m)] = gat[rows, n].T
            for job in range(2):
                for d in range(2):
                    spread(job, m, d).start()

            @pl.when(s < 2)
            def _():
                for n in columns:
                    lt[n, rows] = po[rows, n].T

            @pl.when(s >= 2)
            def _():
                for n in columns:
                    lt[n, rows] = sk[rows, n].T

        @pl.when((i >= 1 + 2 * on3) & (i <= 2 + on3))
        def _():
            forward(i - 1 - 2 * on3)

    @pl.when(s == 3)
    def _():
        forward(1)

    @pl.when(s >= 2)
    def _():
        product(dpre)

    def gathered(job):
        for m in range(2):
            for d in range(2):
                relay(job, m, d).wait_recv()
            for by in (1, 2, 3):
                turned(job, m, by).wait_recv()

    gathered(1)
    block_product(1)
    for block in BLOCKS:
        _, col, width, colour, by = block
        cols = pl.ds(col, width)
        first(block, 0).wait_recv()
        r1[:, :, cols] = (
            r1[:, :, cols].astype(F32) + piece(block, here[colour] + by + 4)[...].astype(F32)
        ).astype(BF16)
        first(block, 1).start()
    gathered(0)
    block_product(0)
    for job in (1, 0):
        for half in range(2):
            o = pl.ds(2 * half, 2)
            sums(job, half, 0).wait_recv()
            pos = (here[1 - job] + 5 - 2 * half) % 4
            p1[job, o] = (p1[job, o].astype(F32) + part[job, o, pos].astype(F32)).astype(BF16)
            sums(job, half, 1).start()
    for block in BLOCKS:
        _, col, width, colour, by = block
        cols = pl.ds(col, width)
        first(block, 1).wait_recv()
        first(block, 2).wait_recv()
        s1[:, :, cols] = (
            piece(block, here[colour])[...].astype(F32)
            + r2[:, :, cols].astype(F32)
            + r3[:, :, cols].astype(F32)
        ).astype(BF16)
        second(block, 0).start()
        second(block, 2).start()
    for job in (1, 0):
        for half in range(2):
            sums(job, half, 1).wait_recv()
            sums(job, half, 2).wait_recv()
            for o in (2 * half, 2 * half + 1):
                total = (
                    part[job, o, here[1 - job]].astype(F32)
                    + p2[job, o].astype(F32)
                    + p3[job, o].astype(F32)
                )
                hs[job, 0, o] = total[:40].astype(BF16)
                hs[job, 1, o] = total[40:].astype(BF16)
        pair(job).start()
    for block in BLOCKS:
        _, col, width, colour, by = block
        cols = pl.ds(col, width)
        second(block, 0).wait_recv()
        pos = (here[1 - colour] + by + 4) % 4
        q1[:, cols] = (q1[:, cols].astype(F32) + s1[pos, :, cols].astype(F32)).astype(BF16)
        second(block, 1).start()
    for job in (1, 0):
        pair(job).wait_recv()
        for o in range(4):
            fs[job, o] = (hs[job, xh, o].astype(F32) + hr[job, o].astype(F32)).astype(BF16)
        for by in (1, 3, 2):
            last(job, by).start()
        fr[job, here[job]] = fs[job, here[job]]
    for block in BLOCKS:
        _, col, width, colour, by = block
        cols = pl.ds(col, width)
        second(block, 1).wait_recv()
        second(block, 2).wait_recv()
        total = (
            s1[here[1 - colour], :, cols].astype(F32)
            + q2[:, cols].astype(F32)
            + q3[:, cols].astype(F32)
        )
        xs[0, :, cols] = total[:40].astype(BF16)
        xs[1, :, cols] = total[40:].astype(BF16)
    pair(2).start()
    for job in (1, 0):
        for by in (1, 2, 3):
            last(job, by).wait_recv()
        for q in range(4):
            (g_in, g_out)[job][:, q * Q : (q + 1) * Q] = fr[job, q].astype(F32)
    pair(2).wait_recv()
    g_skip[...] = xs[xh].astype(F32) + xr[...].astype(F32)
    for block in BLOCKS:
        for msg in range(3):
            first(block, msg).wait_send()
            second(block, msg).wait_send()
    for k in range(3):
        pair(k).wait_send()
    for job in range(2):
        for n in range(3):
            last(job, n + 1).wait_send()
            for m in range(2):
                turned(job, m, n + 1).wait_send()
                sums(job, m, n).wait_send()
        for m in range(2):
            for d in range(2):
                spread(job, m, d).wait_send()
                relay(job, m, d).wait_send()
    for m in range(2):

        @pl.when((s == 0) | (s == 2))
        def _():
            send_x(m).wait_send()

        @pl.when(s == 0)
        def _():
            send_sk(m).wait_send()

        @pl.when(s > 0)
        def _():
            send_up(m).wait_send()

        @pl.when(s >= 2)
        def _():
            send_dk(m).wait_send()


def deliver(*refs):
    sem = refs[-1]
    copies = [pltpu.make_async_copy(refs[n], refs[5 + n], sem.at[n]) for n in range(5)]
    for copy in copies:
        copy.start()
    for copy in copies:
        copy.wait()


def body(latents, cotangent, timesteps, time_table, w_in, w_out, w_skip):
    rows = 2 * R
    vmem = pl.BlockSpec(memory_space=pltpu.VMEM)
    hbm = pl.BlockSpec(memory_space=pltpu.HBM)
    act = pltpu.VMEM((rows, C), BF16)
    weight = pltpu.VMEM((C, C), BF16)
    quarter = pltpu.VMEM((4, 80, C), BF16)
    sixteenth = pltpu.VMEM((80, C), BF16)
    sums = pltpu.VMEM((2, 4, 80, Q), BF16)
    halves = pltpu.VMEM((2, 4, 40, Q), BF16)
    dma = pltpu.SemaphoreType.DMA
    out_act = jax.ShapeDtypeStruct((rows, C), BF16)
    out_grad = jax.ShapeDtypeStruct((40, C), F32)
    outs = (out_act, out_act, out_grad, out_grad, out_grad)
    results = pl.pallas_call(
        kernel,
        name="window",
        out_shape=outs,
        in_specs=[hbm, hbm, pl.BlockSpec(memory_space=pltpu.SMEM), hbm, hbm, hbm, hbm],
        out_specs=[vmem] * 5,
        scratch_shapes=[
            weight, weight, weight,
            pltpu.VMEM((1000, C), BF16),
            pltpu.VMEM((2, 1, C), F32),
            pltpu.VMEM((R, C), F32),
            act, act, act, act,
            pltpu.VMEM((rows, C), F32),
            act, act, act,
            pltpu.VMEM((C, rows), BF16),
            pltpu.VMEM((4, 4, 80, C), BF16),
            quarter, quarter, quarter, quarter,
            sixteenth, sixteenth, sixteenth,
            pltpu.VMEM((2, 40, C), BF16),
            pltpu.VMEM((40, C), BF16),
            pltpu.VMEM((2, C, 4 * rows), BF16),
            pltpu.VMEM((2, 4, rows, Q), BF16),
            pltpu.VMEM((2, 4 * rows, Q), BF16),
            pltpu.VMEM((2, 4, 4, 80, Q), BF16),
            sums, sums, sums,
            pltpu.VMEM((2, 2, 4, 40, Q), BF16),
            halves, halves, halves,
            dma((4,)),
            pltpu.SemaphoreType.REGULAR,
            dma((2,)), dma((3,)),
            dma((2,)), dma((2,)),
            dma((2,)), dma((3,)),
            dma((2,)), dma((2,)),
            dma((2, 3, 4)), dma((2, 3, 4)),
            dma((3,)), dma((3,)),
            dma((2, 2, 2)), dma((2, 2, 2)),
            dma((2, 2, 2)), dma((2, 2, 2)),
            dma((2, 2, 3)), dma((2, 2, 3)),
            dma((2, 2, 3)), dma((2, 2, 3)),
            dma((2, 3)), dma((2, 3)),
        ],
        compiler_params=pltpu.CompilerParams(
            collective_id=0, has_side_effects=True, vmem_limit_bytes=54_000_000
        ),
    )(
        latents.reshape(rows, C), cotangent.reshape(rows, C), timesteps.reshape(2), time_table.reshape(1000, C),
        w_in.reshape(C, C), w_out.reshape(C, C), w_skip.reshape(C, C),
    )
    po, gi, g_in, g_out, g_skip = pl.pallas_call(
        deliver,
        name="deliver",
        out_shape=outs,
        in_specs=[vmem] * 5,
        out_specs=[hbm] * 5,
        scratch_shapes=[dma((5,))],
        compiler_params=pltpu.CompilerParams(vmem_limit_bytes=4_000_000),
    )(*results)
    return (
        po.reshape(1, 2, R, C),
        gi.reshape(1, 2, R, C),
        g_in[None],
        g_out[None],
        g_skip[None],
    )


def solution(mesh):
    in_specs = (
        P(None, "dp", None),
        P(None, "dp", None),
        P(None, "dp"),
        P("segment", None, None),
        P("segment", None, None),
        P("segment", None, None),
        P("segment", None, None),
    )
    out_specs = (
        P("segment", None, "dp", None),
        P("segment", None, "dp", None),
        P("segment", "dp", None),
        P("segment", "dp", None),
        P("segment", "dp", None),
    )
    return jax.shard_map(body, mesh=mesh, in_specs=in_specs, out_specs=out_specs, check_vma=False)
```

```python
import jax
import jax.numpy as jnp
from jax import lax
from jax.experimental import pallas as pl
from jax.experimental.pallas import tpu as pltpu
from jax.sharding import PartitionSpec as P

MESH = pl.DeviceIdType.MESH
F32 = jnp.float32
BF16 = jnp.bfloat16
C = 1280
R = 128
TILE = 256
BLOCKS = ((0, 0, 384, 0, 1), (1, 384, 256, 0, -1), (2, 640, 256, 1, 1), (3, 896, 384, 1, -1))
Q = C // 4


def kernel(
    lat, cot, steps, table, w_in, w_out, w_skip,
    po, gi, g_in, g_out, g_skip,
    w1, w2, w3, wt, rows_t, bias, acc, x, up, sk, dk, pre, gat, tot, dpre, lt, grads, r1, r2, r3, s1, q1, q2, q3, xs, xr,
    left, stage, right, part, p1, p2, p3, hs, hr, fs, fr,
    wsem, turn, x_s, x_r, sk_s, sk_r, up_s, up_r, dk_s, dk_r, rs_s, rs_r, xh_s, xh_r,
    ag_s, ag_r, fw_s, fw_r, aa_s, aa_r, js_s, js_r, fin_s, fin_r,
):
    s = lax.axis_index("segment")
    dp = lax.axis_index("dp")
    z = dp // 8
    y = (dp // 2) % 4
    xh = dp % 2

    def along(axis, by):
        if axis == 0:
            return ((z + by + 4) % 4) * 8 + y * 2 + xh
        return z * 8 + ((y + by + 4) % 4) * 2 + xh

    partner = z * 8 + y * 2 + (1 - xh)
    loads = [
        pltpu.make_async_copy(src, dst, wsem.at[n])
        for n, (src, dst) in enumerate(((w_in, w1), (table, rows_t), (w_out, w2), (w_skip, w3)))
    ]
    x_load = pltpu.make_async_copy(lat, x, x_r.at[2])
    up_load = pltpu.make_async_copy(cot, up, up_r.at[2])

    @pl.when(s == 0)
    def _():
        x_load.start()

    for load in loads:
        load.start()

    @pl.when(s == 3)
    def _():
        up_load.start()

    barrier = pltpu.get_barrier_semaphore()
    for by in (1, 2, 3):
        pl.semaphore_signal(barrier, inc=1, device_id={"segment": (s + by) % 4}, device_id_type=MESH)
    for other in [along(axis, by) for axis in (0, 1) for by in (1, 2, 3)] + [partner]:
        pl.semaphore_signal(barrier, inc=1, device_id={"dp": other}, device_id_type=MESH)

    def hand(buf, dst, m, send, recv, to):
        rows = pl.ds(pl.multiple_of(m * R, R), R)
        return pltpu.make_async_remote_copy(
            src_ref=buf.at[rows], dst_ref=dst.at[rows], send_sem=send.at[m], recv_sem=recv.at[m],
            device_id={"segment": to}, device_id_type=MESH,
        )

    def send_x(m):
        return hand(po, x, m, x_s, x_r, (s + 1) % 4)

    def send_sk(m):
        return hand(sk, sk, m, sk_s, sk_r, 3 - s)

    def send_up(m):
        return hand(gi, up, m, up_s, up_r, (s + 3) % 4)

    def send_dk(m):
        return hand(dk, dk, m, dk_s, dk_r, 3 - s)

    columns = [pl.ds(n * TILE, TILE) for n in range(C // TILE)]
    on3 = s // 3

    here = (z, y)

    def ring(step, msg, block, src, dst, axis, by):
        n = block[0]
        return pltpu.make_async_remote_copy(
            src_ref=src, dst_ref=dst, send_sem=rs_s.at[step, msg, n], recv_sem=rs_r.at[step, msg, n],
            device_id={"dp": along(axis, by)}, device_id_type=MESH,
        )

    def piece(block, pos):
        _, col, width, colour, _ = block
        cols = pl.ds(col, width)
        if colour == 0:
            return grads.at[pos % 4, :, :, cols]
        return grads.at[:, pos % 4, :, cols]

    def first(block, msg):
        _, col, width, colour, by = block
        cols = pl.ds(col, width)
        pos = here[colour]
        if msg == 0:
            return ring(0, 0, block, piece(block, pos + 2), r1.at[:, :, cols], colour, by)
        if msg == 1:
            return ring(0, 1, block, r1.at[:, :, cols], r2.at[:, :, cols], colour, by)
        return ring(0, 2, block, piece(block, pos - by + 4), r3.at[:, :, cols], colour, -by)

    def second(block, msg):
        _, col, width, colour, by = block
        cols = pl.ds(col, width)
        axis = 1 - colour
        pos = here[axis]
        if msg == 0:
            return ring(1, 0, block, s1.at[(pos + 2) % 4, :, cols], q1.at[:, cols], axis, by)
        if msg == 1:
            return ring(1, 1, block, q1.at[:, cols], q2.at[:, cols], axis, by)
        return ring(1, 2, block, s1.at[(pos - by + 4) % 4, :, cols], q3.at[:, cols], axis, -by)

    def product(other):
        for n in columns:
            whole = jnp.dot(lt[...], other[:, n], preferred_element_type=F32).astype(BF16)
            for j in range(16):
                grads[j // 4, j % 4, :, n] = whole[j * 80 : (j + 1) * 80]

        for block in BLOCKS:
            first(block, 0).start()
            first(block, 2).start()

    def remote(src, dst, send, recv, axis, by):
        return pltpu.make_async_remote_copy(
            src_ref=src, dst_ref=dst, send_sem=send, recv_sem=recv,
            device_id={"dp": along(axis, by)}, device_id_type=MESH,
        )

    def slot(job, m, by=0):
        return pl.ds(pl.multiple_of(((here[job] + by + 4) % 4 * 2 + m) * R, R), R)

    def spread(job, m, d):
        ref = left.at[job, :, slot(job, m)]
        return remote(ref, ref, ag_s.at[job, m, d], ag_r.at[job, m, d], job, 1 - 2 * d)

    def relay(job, m, d):
        by = 1 - 2 * d
        ref = left.at[job, pl.ds(d * 640, 640), slot(job, m, -by)]
        return remote(ref, ref, fw_s.at[job, m, d], fw_r.at[job, m, d], job, by)

    def forward(m):
        for job in range(2):
            for d in range(2):
                spread(job, m, d).wait_recv()
                relay(job, m, d).start()

    def turned(job, m, by):
        rows = pl.ds(pl.multiple_of(m * R, R), R)
        return remote(
            stage.at[job, (here[job] + by) % 4, rows], right.at[job, slot(job, m)],
            aa_s.at[job, m, by - 1], aa_r.at[job, m, by - 1], job, by,
        )

    def swap(job, m):
        rows = pl.ds(pl.multiple_of(m * R, R), R)
        value = (dpre, tot)[job]
        for q in range(4):
            stage[job, q, rows, :] = value[rows, q * Q : (q + 1) * Q]
        for by in (1, 3, 2):
            turned(job, m, by).start()
        right[job, slot(job, m), :] = stage[job, here[job], rows, :]

    def sums(job, half, msg):
        by = 1 - 2 * half
        axis = 1 - job
        pos = here[axis]
        o = pl.ds(2 * half, 2)
        sems = (js_s.at[job, half, msg], js_r.at[job, half, msg])
        if msg == 0:
            return remote(part.at[job, o, (pos + 2) % 4], p1.at[job, o], *sems, axis, by)
        if msg == 1:
            return remote(p1.at[job, o], p2.at[job, o], *sems, axis, by)
        return remote(part.at[job, o, (pos - by + 4) % 4], p3.at[job, o], *sems, axis, -by)

    def block_product(job):
        whole = jnp.dot(left[job], right[job], preferred_element_type=F32).astype(BF16)
        for j in range(16):
            at = (j // 4, j % 4) if job == 0 else (j % 4, j // 4)
            part[job, *at] = whole[j * 80 : (j + 1) * 80]

        for half in range(2):
            sums(job, half, 0).start()
            sums(job, half, 2).start()

    def pair(k):
        src, dst = ((hs.at[0, 1 - xh], hr.at[0]), (hs.at[1, 1 - xh], hr.at[1]), (xs.at[1 - xh], xr))[k]
        return pltpu.make_async_remote_copy(
            src_ref=src, dst_ref=dst, send_sem=xh_s.at[k], recv_sem=xh_r.at[k],
            device_id={"dp": partner}, device_id_type=MESH,
        )

    def last(job, by):
        return remote(
            fs.at[job, (here[job] + by) % 4], fr.at[job, here[job]],
            fin_s.at[job, by - 1], fin_r.at[job, by - 1], job, by,
        )

    @pl.loop(0, 4)
    def _(i):
        kind = on3 * (i % 2) + (1 - on3) * (i // 2)
        m = on3 * (i // 2) + (1 - on3) * (i % 2)
        rows = pl.ds(pl.multiple_of(m * R, R), R)

        @pl.when((i == 0) & (s >= 2))
        def _():
            for n in (0, 2, 3):
                loads[n].wait()

        @pl.when(i == 2 * (1 - s // 2))
        def _():
            @pl.loop(0, C // TILE)
            def _(j):
                span = pl.ds(pl.multiple_of(j * TILE, TILE), TILE)
                for k, w in enumerate((w1, w2, w3)):
                    for n in columns:
                        wt[k, n, span] = w[span, n].T

        @pl.when(kind == 0)
        def _():
            @pl.when((s == 0) & (m == 0))
            def _():
                x_load.wait()

            @pl.when(s > 0)
            def _():
                send_x(m).wait_recv()

            @pl.when((i == 0) & (s < 2))
            def _():
                loads[0].wait()

            for n in columns:
                pre[rows, n] = jnp.dot(x[rows, :], w1[:, n], preferred_element_type=F32)

            @pl.when(i == 0)
            def _():
                loads[1].wait()
                row = lax.broadcasted_iota(jnp.int32, (8, table.shape[0]), 0)
                chosen = jnp.where(row == 0, steps[0], steps[1])
                hot = lax.broadcasted_iota(jnp.int32, (8, table.shape[0]), 1) == chosen
                found = jnp.dot(hot.astype(F32).astype(BF16), rows_t[...], preferred_element_type=F32)
                bias[0] = found[0:1]
                bias[1] = found[1:2]

                @pl.when(s < 2)
                def _():
                    loads[2].wait()
                    loads[3].wait()

            @pl.when(s >= 2)
            def _():
                send_sk(m).wait_recv()
                for n in columns:
                    pre[rows, n] += jnp.dot(sk[rows, :], w3[:, n], preferred_element_type=F32)

            for n in columns:
                v = pre[rows, n] + bias[m, :, n]
                g = 1.0 / (1.0 + jnp.exp(-v))
                gat[rows, n] = (v * g).astype(BF16)
                pre[rows, n] = g * (1.0 + v * (1.0 - g))
            for n in columns:
                po[rows, n] = (
                    x[rows, n].astype(F32)
                    + jnp.dot(gat[rows, :], w2[:, n], preferred_element_type=F32)
                ).astype(BF16)

            @pl.when(i == 0)
            def _():
                pl.semaphore_wait(barrier, 10)

            @pl.when(s < 3)
            def _():
                send_x(m).start()

            @pl.when(s < 2)
            def _():
                for n in columns:
                    sk[rows, n] = jnp.dot(
                        po[rows, :], w3[:, n], preferred_element_type=F32
                    ).astype(BF16)

                @pl.when(s == 1)
                def _():
                    send_sk(m).start()

                    @pl.when(m == 1)
                    def _():
                        for j in range(2):
                            send_x(j).wait_send()
                            send_sk(j).wait_send()
                        pl.semaphore_signal(turn, inc=1, device_id={"segment": 0}, device_id_type=MESH)

                @pl.when(s == 0)
                def _():
                    @pl.when(m == 1)
                    def _():
                        pl.semaphore_wait(turn, 1)

                    send_sk(m).start()

        @pl.when(kind == 1)
        def _():
            @pl.when((s == 3) & (m == 0))
            def _():
                up_load.wait()

            @pl.when(s < 2)
            def _():
                send_dk(m).wait_recv()
                for n in columns:
                    acc[:, n] = jnp.dot(dk[rows, :], wt[2, :, n], preferred_element_type=F32)

                @pl.when(m == 1)
                def _():
                    product(dk)

            @pl.when(s < 3)
            def _():
                send_up(m).wait_recv()

            @pl.when(s < 2)
            def _():
                tot[rows, :] = (up[rows, :].astype(F32) + acc[...]).astype(BF16)

            @pl.when(s >= 2)
            def _():
                tot[rows, :] = up[rows, :]

            for n in columns:
                dpre[rows, n] = (
                    jnp.dot(tot[rows, :], wt[1, :, n], preferred_element_type=F32)
                    * pre[rows, n]
                ).astype(BF16)

            @pl.when(s == 0)
            def _():
                swap(1, m)
                swap(0, m)

            @pl.when(s == 2)
            def _():
                for n in columns:
                    dk[rows, n] = jnp.dot(
                        dpre[rows, :], wt[2, :, n], preferred_element_type=F32
                    ).astype(BF16)
                send_dk(m).start()

            for n in columns:
                gi[rows, n] = (
                    tot[rows, n].astype(F32)
                    + jnp.dot(dpre[rows, :], wt[0, :, n], preferred_element_type=F32)
                ).astype(BF16)

            @pl.when(s > 0)
            def _():
                send_up(m).start()

            @pl.when(s == 3)
            def _():
                for n in columns:
                    dk[rows, n] = jnp.dot(
                        dpre[rows, :], wt[2, :, n], preferred_element_type=F32
                    ).astype(BF16)
                send_dk(m).start()

            @pl.when(s > 0)
            def _():
                swap(1, m)
                swap(0, m)

        @pl.when(kind == on3)
        def _():
            for n in columns:
                left[0, n, slot(0, m)] = x[rows, n].T
                left[1, n, slot(1, m)] = gat[rows, n].T
            for job in range(2):
                for d in range(2):
                    spread(job, m, d).start()

            @pl.when(s < 2)
            def _():
                for n in columns:
                    lt[n, rows] = po[rows, n].T

            @pl.when(s >= 2)
            def _():
                for n in columns:
                    lt[n, rows] = sk[rows, n].T

        @pl.when((i >= 1 + 2 * on3) & (i <= 2 + on3))
        def _():
            forward(i - 1 - 2 * on3)

    @pl.when(s == 3)
    def _():
        forward(1)

    @pl.when(s >= 2)
    def _():
        product(dpre)

    def gathered(job):
        for m in range(2):
            for d in range(2):
                relay(job, m, d).wait_recv()
            for by in (1, 2, 3):
                turned(job, m, by).wait_recv()

    for block in BLOCKS:
        _, col, width, colour, by = block
        cols = pl.ds(col, width)
        first(block, 0).wait_recv()
        r1[:, :, cols] = (
            r1[:, :, cols].astype(F32) + piece(block, here[colour] + by + 4)[...].astype(F32)
        ).astype(BF16)
        first(block, 1).start()
    for block in BLOCKS:
        _, col, width, colour, by = block
        cols = pl.ds(col, width)
        first(block, 1).wait_recv()
        first(block, 2).wait_recv()
        s1[:, :, cols] = (
            piece(block, here[colour])[...].astype(F32)
            + r2[:, :, cols].astype(F32)
            + r3[:, :, cols].astype(F32)
        ).astype(BF16)
        second(block, 0).start()
        second(block, 2).start()
    gathered(1)
    block_product(1)
    gathered(0)
    block_product(0)
    for job in (1, 0):
        for half in range(2):
            o = pl.ds(2 * half, 2)
            sums(job, half, 0).wait_recv()
            pos = (here[1 - job] + 5 - 2 * half) % 4
            p1[job, o] = (p1[job, o].astype(F32) + part[job, o, pos].astype(F32)).astype(BF16)
            sums(job, half, 1).start()
    for job in (1, 0):
        for half in range(2):
            sums(job, half, 1).wait_recv()
            sums(job, half, 2).wait_recv()
            for o in (2 * half, 2 * half + 1):
                total = (
                    part[job, o, here[1 - job]].astype(F32)
                    + p2[job, o].astype(F32)
                    + p3[job, o].astype(F32)
                )
                hs[job, 0, o] = total[:40].astype(BF16)
                hs[job, 1, o] = total[40:].astype(BF16)
        pair(job).start()
    for block in BLOCKS:
        _, col, width, colour, by = block
        cols = pl.ds(col, width)
        second(block, 0).wait_recv()
        pos = (here[1 - colour] + by + 4) % 4
        q1[:, cols] = (q1[:, cols].astype(F32) + s1[pos, :, cols].astype(F32)).astype(BF16)
        second(block, 1).start()
    for job in (1, 0):
        pair(job).wait_recv()
        for o in range(4):
            fs[job, o] = (hs[job, xh, o].astype(F32) + hr[job, o].astype(F32)).astype(BF16)
        for by in (1, 3, 2):
            last(job, by).start()
        fr[job, here[job]] = fs[job, here[job]]
    for block in BLOCKS:
        _, col, width, colour, by = block
        cols = pl.ds(col, width)
        second(block, 1).wait_recv()
        second(block, 2).wait_recv()
        total = (
            s1[here[1 - colour], :, cols].astype(F32)
            + q2[:, cols].astype(F32)
            + q3[:, cols].astype(F32)
        )
        xs[0, :, cols] = total[:40].astype(BF16)
        xs[1, :, cols] = total[40:].astype(BF16)
    pair(2).start()
    for job in (1, 0):
        for by in (1, 2, 3):
            last(job, by).wait_recv()
        for q in range(4):
            (g_in, g_out)[job][:, q * Q : (q + 1) * Q] = fr[job, q].astype(F32)
    pair(2).wait_recv()
    g_skip[...] = xs[xh].astype(F32) + xr[...].astype(F32)
    for block in BLOCKS:
        for msg in range(3):
            first(block, msg).wait_send()
            second(block, msg).wait_send()
    for k in range(3):
        pair(k).wait_send()
    for job in range(2):
        for n in range(3):
            last(job, n + 1).wait_send()
            for m in range(2):
                turned(job, m, n + 1).wait_send()
                sums(job, m, n).wait_send()
        for m in range(2):
            for d in range(2):
                spread(job, m, d).wait_send()
                relay(job, m, d).wait_send()
    for m in range(2):

        @pl.when((s == 0) | (s == 2))
        def _():
            send_x(m).wait_send()

        @pl.when(s == 0)
        def _():
            send_sk(m).wait_send()

        @pl.when(s > 0)
        def _():
            send_up(m).wait_send()

        @pl.when(s >= 2)
        def _():
            send_dk(m).wait_send()


def deliver(*refs):
    sem = refs[-1]
    copies = [pltpu.make_async_copy(refs[n], refs[5 + n], sem.at[n]) for n in range(5)]
    for copy in copies:
        copy.start()
    for copy in copies:
        copy.wait()


def body(latents, cotangent, timesteps, time_table, w_in, w_out, w_skip):
    rows = 2 * R
    vmem = pl.BlockSpec(memory_space=pltpu.VMEM)
    hbm = pl.BlockSpec(memory_space=pltpu.HBM)
    act = pltpu.VMEM((rows, C), BF16)
    weight = pltpu.VMEM((C, C), BF16)
    quarter = pltpu.VMEM((4, 80, C), BF16)
    sixteenth = pltpu.VMEM((80, C), BF16)
    sums = pltpu.VMEM((2, 4, 80, Q), BF16)
    halves = pltpu.VMEM((2, 4, 40, Q), BF16)
    dma = pltpu.SemaphoreType.DMA
    out_act = jax.ShapeDtypeStruct((rows, C), BF16)
    out_grad = jax.ShapeDtypeStruct((40, C), F32)
    outs = (out_act, out_act, out_grad, out_grad, out_grad)
    results = pl.pallas_call(
        kernel,
        name="window",
        out_shape=outs,
        in_specs=[hbm, hbm, pl.BlockSpec(memory_space=pltpu.SMEM), hbm, hbm, hbm, hbm],
        out_specs=[vmem] * 5,
        scratch_shapes=[
            weight, weight, weight,
            pltpu.VMEM((3, C, C), BF16),
            pltpu.VMEM((1000, C), BF16),
            pltpu.VMEM((2, 1, C), F32),
            pltpu.VMEM((R, C), F32),
            act, act, act, act,
            pltpu.VMEM((rows, C), F32),
            act, act, act,
            pltpu.VMEM((C, rows), BF16),
            pltpu.VMEM((4, 4, 80, C), BF16),
            quarter, quarter, quarter, quarter,
            sixteenth, sixteenth, sixteenth,
            pltpu.VMEM((2, 40, C), BF16),
            pltpu.VMEM((40, C), BF16),
            pltpu.VMEM((2, C, 4 * rows), BF16),
            pltpu.VMEM((2, 4, rows, Q), BF16),
            pltpu.VMEM((2, 4 * rows, Q), BF16),
            pltpu.VMEM((2, 4, 4, 80, Q), BF16),
            sums, sums, sums,
            pltpu.VMEM((2, 2, 4, 40, Q), BF16),
            halves, halves, halves,
            dma((4,)),
            pltpu.SemaphoreType.REGULAR,
            dma((2,)), dma((3,)),
            dma((2,)), dma((2,)),
            dma((2,)), dma((3,)),
            dma((2,)), dma((2,)),
            dma((2, 3, 4)), dma((2, 3, 4)),
            dma((3,)), dma((3,)),
            dma((2, 2, 2)), dma((2, 2, 2)),
            dma((2, 2, 2)), dma((2, 2, 2)),
            dma((2, 2, 3)), dma((2, 2, 3)),
            dma((2, 2, 3)), dma((2, 2, 3)),
            dma((2, 3)), dma((2, 3)),
        ],
        compiler_params=pltpu.CompilerParams(
            collective_id=0, has_side_effects=True, vmem_limit_bytes=54_000_000
        ),
    )(
        latents.reshape(rows, C), cotangent.reshape(rows, C), timesteps.reshape(2), time_table.reshape(1000, C),
        w_in.reshape(C, C), w_out.reshape(C, C), w_skip.reshape(C, C),
    )
    po, gi, g_in, g_out, g_skip = pl.pallas_call(
        deliver,
        name="deliver",
        out_shape=outs,
        in_specs=[vmem] * 5,
        out_specs=[hbm] * 5,
        scratch_shapes=[dma((5,))],
        compiler_params=pltpu.CompilerParams(vmem_limit_bytes=4_000_000),
    )(*results)
    return (
        po.reshape(1, 2, R, C),
        gi.reshape(1, 2, R, C),
        g_in[None],
        g_out[None],
        g_skip[None],
    )


def solution(mesh):
    in_specs = (
        P(None, "dp", None),
        P(None, "dp", None),
        P(None, "dp"),
        P("segment", None, None),
        P("segment", None, None),
        P("segment", None, None),
        P("segment", None, None),
    )
    out_specs = (
        P("segment", None, "dp", None),
        P("segment", None, "dp", None),
        P("segment", "dp", None),
        P("segment", "dp", None),
        P("segment", "dp", None),
    )
    return jax.shard_map(body, mesh=mesh, in_specs=in_specs, out_specs=out_specs, check_vma=False)
```

```python
import jax
import jax.numpy as jnp
from jax import lax
from jax.experimental import pallas as pl
from jax.experimental.pallas import tpu as pltpu
from jax.sharding import PartitionSpec as P

MESH = pl.DeviceIdType.MESH
F32 = jnp.float32
BF16 = jnp.bfloat16
C = 1280
R = 128
TILE = 256
BLOCKS = ((0, 0, 384, 0, 1), (1, 384, 256, 0, -1), (2, 640, 256, 1, 1), (3, 896, 384, 1, -1))
Q = C // 4
WIDE = 384


def kernel(
    lat, cot, steps, table, w_in, w_out, w_skip,
    po, gi, g_in, g_out, g_skip,
    w1, w2, w3, wt, rows_t, bias, acc, x, up, sk, dk, pre, gat, tot, dpre, lt, grads, r1, r2, r3, s1, q1, q2, q3, xs, xr,
    left, stage, right, part, p1, p2, p3, hs, hr, fs, fr,
    wsem, turn, x_s, x_r, sk_s, sk_r, up_s, up_r, dk_s, dk_r, rs_s, rs_r, xh_s, xh_r,
    ag_s, ag_r, fw_s, fw_r, aa_s, aa_r, js_s, js_r, fin_s, fin_r,
):
    s = lax.axis_index("segment")
    dp = lax.axis_index("dp")
    z = dp // 8
    y = (dp // 2) % 4
    xh = dp % 2

    def along(axis, by):
        if axis == 0:
            return ((z + by + 4) % 4) * 8 + y * 2 + xh
        return z * 8 + ((y + by + 4) % 4) * 2 + xh

    partner = z * 8 + y * 2 + (1 - xh)
    loads = [
        pltpu.make_async_copy(src, dst, wsem.at[n])
        for n, (src, dst) in enumerate(((w_in, w1), (table, rows_t), (w_out, w2), (w_skip, w3)))
    ]
    x_load = pltpu.make_async_copy(lat, x, x_r.at[2])
    up_load = pltpu.make_async_copy(cot, up, up_r.at[2])

    @pl.when(s == 0)
    def _():
        x_load.start()

    for load in loads:
        load.start()

    @pl.when(s == 3)
    def _():
        up_load.start()

    barrier = pltpu.get_barrier_semaphore()
    for by in (1, 2, 3):
        pl.semaphore_signal(barrier, inc=1, device_id={"segment": (s + by) % 4}, device_id_type=MESH)
    for other in [along(axis, by) for axis in (0, 1) for by in (1, 2, 3)] + [partner]:
        pl.semaphore_signal(barrier, inc=1, device_id={"dp": other}, device_id_type=MESH)

    def hand(buf, dst, m, send, recv, to):
        rows = pl.ds(pl.multiple_of(m * R, R), R)
        return pltpu.make_async_remote_copy(
            src_ref=buf.at[rows], dst_ref=dst.at[rows], send_sem=send.at[m], recv_sem=recv.at[m],
            device_id={"segment": to}, device_id_type=MESH,
        )

    def send_x(m):
        return hand(po, x, m, x_s, x_r, (s + 1) % 4)

    def send_sk(m):
        return hand(sk, sk, m, sk_s, sk_r, 3 - s)

    def send_up(m):
        return hand(gi, up, m, up_s, up_r, (s + 3) % 4)

    def send_dk(m):
        return hand(dk, dk, m, dk_s, dk_r, 3 - s)

    columns = [pl.ds(n * TILE, TILE) for n in range(C // TILE)]
    on3 = s // 3

    here = (z, y)

    def ring(step, msg, block, src, dst, axis, by):
        n = block[0]
        return pltpu.make_async_remote_copy(
            src_ref=src, dst_ref=dst, send_sem=rs_s.at[step, msg, n], recv_sem=rs_r.at[step, msg, n],
            device_id={"dp": along(axis, by)}, device_id_type=MESH,
        )

    def piece(block, pos):
        _, col, width, colour, _ = block
        cols = pl.ds(col, width)
        if colour == 0:
            return grads.at[pos % 4, :, :, cols]
        return grads.at[:, pos % 4, :, cols]

    def first(block, msg):
        _, col, width, colour, by = block
        cols = pl.ds(col, width)
        pos = here[colour]
        if msg == 0:
            return ring(0, 0, block, piece(block, pos + 2), r1.at[:, :, cols], colour, by)
        if msg == 1:
            return ring(0, 1, block, r1.at[:, :, cols], r2.at[:, :, cols], colour, by)
        return ring(0, 2, block, piece(block, pos - by + 4), r3.at[:, :, cols], colour, -by)

    def second(block, msg):
        _, col, width, colour, by = block
        cols = pl.ds(col, width)
        axis = 1 - colour
        pos = here[axis]
        if msg == 0:
            return ring(1, 0, block, s1.at[(pos + 2) % 4, :, cols], q1.at[:, cols], axis, by)
        if msg == 1:
            return ring(1, 1, block, q1.at[:, cols], q2.at[:, cols], axis, by)
        return ring(1, 2, block, s1.at[(pos - by + 4) % 4, :, cols], q3.at[:, cols], axis, -by)

    def product(other):
        for n in columns:
            whole = jnp.dot(lt[...], other[:, n], preferred_element_type=F32).astype(BF16)
            for j in range(16):
                grads[j // 4, j % 4, :, n] = whole[j * 80 : (j + 1) * 80]

        for block in BLOCKS:
            first(block, 0).start()
            first(block, 2).start()

    def remote(src, dst, send, recv, axis, by):
        return pltpu.make_async_remote_copy(
            src_ref=src, dst_ref=dst, send_sem=send, recv_sem=recv,
            device_id={"dp": along(axis, by)}, device_id_type=MESH,
        )

    def slot(job, m, by=0):
        return pl.ds(pl.multiple_of(((here[job] + by + 4) % 4 * 2 + m) * R, R), R)

    def spread(job, m, d):
        ref = left.at[job, :, slot(job, m)]
        return remote(ref, ref, ag_s.at[job, m, d], ag_r.at[job, m, d], job, 1 - 2 * d)

    def relay(job, m, d):
        by = 1 - 2 * d
        ref = left.at[job, pl.ds(d * 640, 640), slot(job, m, -by)]
        return remote(ref, ref, fw_s.at[job, m, d], fw_r.at[job, m, d], job, by)

    def forward(m):
        for job in range(2):
            for d in range(2):
                spread(job, m, d).wait_recv()
                relay(job, m, d).start()

    def turned(job, m, by):
        rows = pl.ds(pl.multiple_of(m * R, R), R)
        return remote(
            stage.at[job, (here[job] + by) % 4, rows], right.at[job, slot(job, m)],
            aa_s.at[job, m, by - 1], aa_r.at[job, m, by - 1], job, by,
        )

    def swap(job, m):
        rows = pl.ds(pl.multiple_of(m * R, R), R)
        value = (dpre, tot)[job]
        for q in range(4):
            stage[job, q, rows, :Q] = value[rows, q * Q : (q + 1) * Q]
            stage[job, q, rows, Q:] = jnp.zeros((R, WIDE - Q), BF16)
        for by in (1, 3, 2):
            turned(job, m, by).start()
        right[job, slot(job, m), :] = stage[job, here[job], rows, :]

    def sums(job, half, msg):
        by = 1 - 2 * half
        axis = 1 - job
        pos = here[axis]
        o = pl.ds(2 * half, 2)
        sems = (js_s.at[job, half, msg], js_r.at[job, half, msg])
        if msg == 0:
            return remote(part.at[job, o, (pos + 2) % 4], p1.at[job, o], *sems, axis, by)
        if msg == 1:
            return remote(p1.at[job, o], p2.at[job, o], *sems, axis, by)
        return remote(part.at[job, o, (pos - by + 4) % 4], p3.at[job, o], *sems, axis, -by)

    def block_product(job):
        whole = jnp.dot(left[job], right[job], preferred_element_type=F32).astype(BF16)
        for j in range(16):
            at = (j // 4, j % 4) if job == 0 else (j % 4, j // 4)
            part[job, *at] = whole[j * 80 : (j + 1) * 80]

        for half in range(2):
            sums(job, half, 0).start()
            sums(job, half, 2).start()

    def pair(k):
        src, dst = ((hs.at[0, 1 - xh], hr.at[0]), (hs.at[1, 1 - xh], hr.at[1]), (xs.at[1 - xh], xr))[k]
        return pltpu.make_async_remote_copy(
            src_ref=src, dst_ref=dst, send_sem=xh_s.at[k], recv_sem=xh_r.at[k],
            device_id={"dp": partner}, device_id_type=MESH,
        )

    def last(job, by):
        return remote(
            fs.at[job, (here[job] + by) % 4], fr.at[job, here[job]],
            fin_s.at[job, by - 1], fin_r.at[job, by - 1], job, by,
        )

    @pl.loop(0, 4)
    def _(i):
        kind = on3 * (i % 2) + (1 - on3) * (i // 2)
        m = on3 * (i // 2) + (1 - on3) * (i % 2)
        rows = pl.ds(pl.multiple_of(m * R, R), R)

        @pl.when((i == 0) & (s >= 2))
        def _():
            for n in (0, 2, 3):
                loads[n].wait()

        @pl.when(i == 2 * (1 - s // 2))
        def _():
            @pl.loop(0, C // TILE)
            def _(j):
                span = pl.ds(pl.multiple_of(j * TILE, TILE), TILE)
                for k, w in enumerate((w1, w2, w3)):
                    for n in columns:
                        wt[k, n, span] = w[span, n].T

        @pl.when(kind == 0)
        def _():
            @pl.when((s == 0) & (m == 0))
            def _():
                x_load.wait()

            @pl.when(s > 0)
            def _():
                send_x(m).wait_recv()

            @pl.when((i == 0) & (s < 2))
            def _():
                loads[0].wait()

            for n in columns:
                pre[rows, n] = jnp.dot(x[rows, :], w1[:, n], preferred_element_type=F32)

            @pl.when(i == 0)
            def _():
                loads[1].wait()
                row = lax.broadcasted_iota(jnp.int32, (8, table.shape[0]), 0)
                chosen = jnp.where(row == 0, steps[0], steps[1])
                hot = lax.broadcasted_iota(jnp.int32, (8, table.shape[0]), 1) == chosen
                found = jnp.dot(hot.astype(F32).astype(BF16), rows_t[...], preferred_element_type=F32)
                bias[0] = found[0:1]
                bias[1] = found[1:2]

                @pl.when(s < 2)
                def _():
                    loads[2].wait()
                    loads[3].wait()

            @pl.when(s >= 2)
            def _():
                send_sk(m).wait_recv()
                for n in columns:
                    pre[rows, n] += jnp.dot(sk[rows, :], w3[:, n], preferred_element_type=F32)

            for n in columns:
                v = pre[rows, n] + bias[m, :, n]
                g = 1.0 / (1.0 + jnp.exp(-v))
                gat[rows, n] = (v * g).astype(BF16)
                pre[rows, n] = g * (1.0 + v * (1.0 - g))
            for n in columns:
                po[rows, n] = (
                    x[rows, n].astype(F32)
                    + jnp.dot(gat[rows, :], w2[:, n], preferred_element_type=F32)
                ).astype(BF16)

            @pl.when(i == 0)
            def _():
                pl.semaphore_wait(barrier, 10)

            @pl.when(s < 3)
            def _():
                send_x(m).start()

            @pl.when(s < 2)
            def _():
                for n in columns:
                    sk[rows, n] = jnp.dot(
                        po[rows, :], w3[:, n], preferred_element_type=F32
                    ).astype(BF16)

                @pl.when(s == 1)
                def _():
                    send_sk(m).start()

                    @pl.when(m == 1)
                    def _():
                        for j in range(2):
                            send_x(j).wait_send()
                            send_sk(j).wait_send()
                        pl.semaphore_signal(turn, inc=1, device_id={"segment": 0}, device_id_type=MESH)

                @pl.when(s == 0)
                def _():
                    @pl.when(m == 1)
                    def _():
                        pl.semaphore_wait(turn, 1)

                    send_sk(m).start()

        @pl.when(kind == 1)
        def _():
            @pl.when((s == 3) & (m == 0))
            def _():
                up_load.wait()

            @pl.when(s < 2)
            def _():
                send_dk(m).wait_recv()
                for n in columns:
                    acc[:, n] = jnp.dot(dk[rows, :], wt[2, :, n], preferred_element_type=F32)

            @pl.when(s < 3)
            def _():
                send_up(m).wait_recv()

            @pl.when(s < 2)
            def _():
                tot[rows, :] = (up[rows, :].astype(F32) + acc[...]).astype(BF16)

            @pl.when(s >= 2)
            def _():
                tot[rows, :] = up[rows, :]

            for n in columns:
                dpre[rows, n] = (
                    jnp.dot(tot[rows, :], wt[1, :, n], preferred_element_type=F32)
                    * pre[rows, n]
                ).astype(BF16)

            @pl.when(s == 0)
            def _():
                swap(1, m)
                swap(0, m)

            @pl.when(s == 2)
            def _():
                for n in columns:
                    dk[rows, n] = jnp.dot(
                        dpre[rows, :], wt[2, :, n], preferred_element_type=F32
                    ).astype(BF16)
                send_dk(m).start()

            for n in columns:
                gi[rows, n] = (
                    tot[rows, n].astype(F32)
                    + jnp.dot(dpre[rows, :], wt[0, :, n], preferred_element_type=F32)
                ).astype(BF16)

            @pl.when(s > 0)
            def _():
                send_up(m).start()

            @pl.when(s == 3)
            def _():
                for n in columns:
                    dk[rows, n] = jnp.dot(
                        dpre[rows, :], wt[2, :, n], preferred_element_type=F32
                    ).astype(BF16)
                send_dk(m).start()

            @pl.when(s > 0)
            def _():
                swap(1, m)
                swap(0, m)

        @pl.when(kind == on3)
        def _():
            for n in columns:
                left[0, n, slot(0, m)] = x[rows, n].T
                left[1, n, slot(1, m)] = gat[rows, n].T
            for job in range(2):
                for d in range(2):
                    spread(job, m, d).start()

            @pl.when(s < 2)
            def _():
                for n in columns:
                    lt[n, rows] = po[rows, n].T

            @pl.when(s >= 2)
            def _():
                for n in columns:
                    lt[n, rows] = sk[rows, n].T

        @pl.when(i == 1 + 2 * on3)
        def _():
            forward(0)

        @pl.when(((i == 1) & (s < 2)) | ((i == 2) & (s == 2)))
        def _():
            forward(1)

    @pl.when(s == 3)
    def _():
        forward(1)

    @pl.when(s < 2)
    def _():
        product(dk)

    @pl.when(s >= 2)
    def _():
        product(dpre)

    def gathered(job):
        for m in range(2):
            for d in range(2):
                relay(job, m, d).wait_recv()
            for by in (1, 2, 3):
                turned(job, m, by).wait_recv()

    gathered(1)
    block_product(1)
    gathered(0)
    block_product(0)
    for job in (1, 0):
        for half in range(2):
            o = pl.ds(2 * half, 2)
            sums(job, half, 0).wait_recv()
            pos = (here[1 - job] + 5 - 2 * half) % 4
            p1[job, o] = (p1[job, o].astype(F32) + part[job, o, pos].astype(F32)).astype(BF16)
            sums(job, half, 1).start()
    for block in BLOCKS:
        _, col, width, colour, by = block
        cols = pl.ds(col, width)
        first(block, 0).wait_recv()
        r1[:, :, cols] = (
            r1[:, :, cols].astype(F32) + piece(block, here[colour] + by + 4)[...].astype(F32)
        ).astype(BF16)
        first(block, 1).start()
    for job in (1, 0):
        for half in range(2):
            sums(job, half, 1).wait_recv()
            sums(job, half, 2).wait_recv()
            for o in (2 * half, 2 * half + 1):
                total = (
                    part[job, o, here[1 - job]].astype(F32)
                    + p2[job, o].astype(F32)
                    + p3[job, o].astype(F32)
                )
                hs[job, 0, o] = total[:40].astype(BF16)
                hs[job, 1, o] = total[40:].astype(BF16)
        pair(job).start()
    for block in BLOCKS:
        _, col, width, colour, by = block
        cols = pl.ds(col, width)
        first(block, 1).wait_recv()
        first(block, 2).wait_recv()
        s1[:, :, cols] = (
            piece(block, here[colour])[...].astype(F32)
            + r2[:, :, cols].astype(F32)
            + r3[:, :, cols].astype(F32)
        ).astype(BF16)
        second(block, 0).start()
        second(block, 2).start()
    for block in BLOCKS:
        _, col, width, colour, by = block
        cols = pl.ds(col, width)
        second(block, 0).wait_recv()
        pos = (here[1 - colour] + by + 4) % 4
        q1[:, cols] = (q1[:, cols].astype(F32) + s1[pos, :, cols].astype(F32)).astype(BF16)
        second(block, 1).start()
    for job in (1, 0):
        pair(job).wait_recv()
        for o in range(4):
            fs[job, o] = (hs[job, xh, o].astype(F32) + hr[job, o].astype(F32)).astype(BF16)
        for by in (1, 3, 2):
            last(job, by).start()
        fr[job, here[job]] = fs[job, here[job]]
    for block in BLOCKS:
        _, col, width, colour, by = block
        cols = pl.ds(col, width)
        second(block, 1).wait_recv()
        second(block, 2).wait_recv()
        total = (
            s1[here[1 - colour], :, cols].astype(F32)
            + q2[:, cols].astype(F32)
            + q3[:, cols].astype(F32)
        )
        xs[0, :, cols] = total[:40].astype(BF16)
        xs[1, :, cols] = total[40:].astype(BF16)
    pair(2).start()
    for job in (1, 0):
        for by in (1, 2, 3):
            last(job, by).wait_recv()
        for q in range(4):
            (g_in, g_out)[job][:, q * Q : (q + 1) * Q] = fr[job, q, :, :Q].astype(F32)
    pair(2).wait_recv()
    g_skip[...] = xs[xh].astype(F32) + xr[...].astype(F32)
    for block in BLOCKS:
        for msg in range(3):
            first(block, msg).wait_send()
            second(block, msg).wait_send()
    for k in range(3):
        pair(k).wait_send()
    for job in range(2):
        for n in range(3):
            last(job, n + 1).wait_send()
            for m in range(2):
                turned(job, m, n + 1).wait_send()
                sums(job, m, n).wait_send()
        for m in range(2):
            for d in range(2):
                spread(job, m, d).wait_send()
                relay(job, m, d).wait_send()
    for m in range(2):

        @pl.when((s == 0) | (s == 2))
        def _():
            send_x(m).wait_send()

        @pl.when(s == 0)
        def _():
            send_sk(m).wait_send()

        @pl.when(s > 0)
        def _():
            send_up(m).wait_send()

        @pl.when(s >= 2)
        def _():
            send_dk(m).wait_send()


def deliver(*refs):
    sem = refs[-1]
    copies = [pltpu.make_async_copy(refs[n], refs[5 + n], sem.at[n]) for n in range(5)]
    for copy in copies:
        copy.start()
    for copy in copies:
        copy.wait()


def body(latents, cotangent, timesteps, time_table, w_in, w_out, w_skip):
    rows = 2 * R
    vmem = pl.BlockSpec(memory_space=pltpu.VMEM)
    hbm = pl.BlockSpec(memory_space=pltpu.HBM)
    act = pltpu.VMEM((rows, C), BF16)
    weight = pltpu.VMEM((C, C), BF16)
    quarter = pltpu.VMEM((4, 80, C), BF16)
    sixteenth = pltpu.VMEM((80, C), BF16)
    sums = pltpu.VMEM((2, 4, 80, WIDE), BF16)
    halves = pltpu.VMEM((2, 4, 40, WIDE), BF16)
    dma = pltpu.SemaphoreType.DMA
    out_act = jax.ShapeDtypeStruct((rows, C), BF16)
    out_grad = jax.ShapeDtypeStruct((40, C), F32)
    outs = (out_act, out_act, out_grad, out_grad, out_grad)
    results = pl.pallas_call(
        kernel,
        name="window",
        out_shape=outs,
        in_specs=[hbm, hbm, pl.BlockSpec(memory_space=pltpu.SMEM), hbm, hbm, hbm, hbm],
        out_specs=[vmem] * 5,
        scratch_shapes=[
            weight, weight, weight,
            pltpu.VMEM((3, C, C), BF16),
            pltpu.VMEM((1000, C), BF16),
            pltpu.VMEM((2, 1, C), F32),
            pltpu.VMEM((R, C), F32),
            act, act, act, act,
            pltpu.VMEM((rows, C), F32),
            act, act, act,
            pltpu.VMEM((C, rows), BF16),
            pltpu.VMEM((4, 4, 80, C), BF16),
            quarter, quarter, quarter, quarter,
            sixteenth, sixteenth, sixteenth,
            pltpu.VMEM((2, 40, C), BF16),
            pltpu.VMEM((40, C), BF16),
            pltpu.VMEM((2, C, 4 * rows), BF16),
            pltpu.VMEM((2, 4, rows, WIDE), BF16),
            pltpu.VMEM((2, 4 * rows, WIDE), BF16),
            pltpu.VMEM((2, 4, 4, 80, WIDE), BF16),
            sums, sums, sums,
            pltpu.VMEM((2, 2, 4, 40, WIDE), BF16),
            halves, halves, halves,
            dma((4,)),
            pltpu.SemaphoreType.REGULAR,
            dma((2,)), dma((3,)),
            dma((2,)), dma((2,)),
            dma((2,)), dma((3,)),
            dma((2,)), dma((2,)),
            dma((2, 3, 4)), dma((2, 3, 4)),
            dma((3,)), dma((3,)),
            dma((2, 2, 2)), dma((2, 2, 2)),
            dma((2, 2, 2)), dma((2, 2, 2)),
            dma((2, 2, 3)), dma((2, 2, 3)),
            dma((2, 2, 3)), dma((2, 2, 3)),
            dma((2, 3)), dma((2, 3)),
        ],
        compiler_params=pltpu.CompilerParams(
            collective_id=0, has_side_effects=True, vmem_limit_bytes=54_000_000
        ),
    )(
        latents.reshape(rows, C), cotangent.reshape(rows, C), timesteps.reshape(2), time_table.reshape(1000, C),
        w_in.reshape(C, C), w_out.reshape(C, C), w_skip.reshape(C, C),
    )
    po, gi, g_in, g_out, g_skip = pl.pallas_call(
        deliver,
        name="deliver",
        out_shape=outs,
        in_specs=[vmem] * 5,
        out_specs=[hbm] * 5,
        scratch_shapes=[dma((5,))],
        compiler_params=pltpu.CompilerParams(vmem_limit_bytes=4_000_000),
    )(*results)
    return (
        po.reshape(1, 2, R, C),
        gi.reshape(1, 2, R, C),
        g_in[None],
        g_out[None],
        g_skip[None],
    )


def solution(mesh):
    in_specs = (
        P(None, "dp", None),
        P(None, "dp", None),
        P(None, "dp"),
        P("segment", None, None),
        P("segment", None, None),
        P("segment", None, None),
        P("segment", None, None),
    )
    out_specs = (
        P("segment", None, "dp", None),
        P("segment", None, "dp", None),
        P("segment", "dp", None),
        P("segment", "dp", None),
        P("segment", "dp", None),
    )
    return jax.shard_map(body, mesh=mesh, in_specs=in_specs, out_specs=out_specs, check_vma=False)
```

```python
import jax
import jax.numpy as jnp
from jax import lax
from jax.experimental import pallas as pl
from jax.experimental.pallas import tpu as pltpu
from jax.sharding import PartitionSpec as P

MESH = pl.DeviceIdType.MESH
F32 = jnp.float32
BF16 = jnp.bfloat16
C = 1280
R = 128
TILE = 256
AXES = (0, 1, 0)
Q = C // 4
WIDE = 384


def kernel(
    lat, cot, steps, table, w_in, w_out, w_skip,
    po, gi, g_in, g_out, g_skip,
    w1, w2, w3, wt, rows_t, bias, acc, x, up, sk, dk, pre, gat, tot, dpre,
    left, stage, right, part, p1, p2, p3, hs, hr, fs, fr,
    wsem, turn, x_s, x_r, sk_s, sk_r, up_s, up_r, dk_s, dk_r, xh_s, xh_r,
    ag_s, ag_r, fw_s, fw_r, aa_s, aa_r, js_s, js_r, fin_s, fin_r,
):
    s = lax.axis_index("segment")
    dp = lax.axis_index("dp")
    z = dp // 8
    y = (dp // 2) % 4
    xh = dp % 2

    def along(axis, by):
        if axis == 0:
            return ((z + by + 4) % 4) * 8 + y * 2 + xh
        return z * 8 + ((y + by + 4) % 4) * 2 + xh

    partner = z * 8 + y * 2 + (1 - xh)
    loads = [
        pltpu.make_async_copy(src, dst, wsem.at[n])
        for n, (src, dst) in enumerate(((w_in, w1), (table, rows_t), (w_out, w2), (w_skip, w3)))
    ]
    x_load = pltpu.make_async_copy(lat, x, x_r.at[2])
    up_load = pltpu.make_async_copy(cot, up, up_r.at[2])

    @pl.when(s == 0)
    def _():
        x_load.start()

    for load in loads:
        load.start()

    @pl.when(s == 3)
    def _():
        up_load.start()

    barrier = pltpu.get_barrier_semaphore()
    for by in (1, 2, 3):
        pl.semaphore_signal(barrier, inc=1, device_id={"segment": (s + by) % 4}, device_id_type=MESH)
    for other in [along(axis, by) for axis in (0, 1) for by in (1, 2, 3)] + [partner]:
        pl.semaphore_signal(barrier, inc=1, device_id={"dp": other}, device_id_type=MESH)

    def hand(buf, dst, m, send, recv, to):
        rows = pl.ds(pl.multiple_of(m * R, R), R)
        return pltpu.make_async_remote_copy(
            src_ref=buf.at[rows], dst_ref=dst.at[rows], send_sem=send.at[m], recv_sem=recv.at[m],
            device_id={"segment": to}, device_id_type=MESH,
        )

    def send_x(m):
        return hand(po, x, m, x_s, x_r, (s + 1) % 4)

    def send_sk(m):
        return hand(sk, sk, m, sk_s, sk_r, 3 - s)

    def send_up(m):
        return hand(gi, up, m, up_s, up_r, (s + 3) % 4)

    def send_dk(m):
        return hand(dk, dk, m, dk_s, dk_r, 3 - s)

    columns = [pl.ds(n * TILE, TILE) for n in range(C // TILE)]
    on3 = s // 3

    here = (z, y)

    def remote(src, dst, send, recv, axis, by):
        return pltpu.make_async_remote_copy(
            src_ref=src, dst_ref=dst, send_sem=send, recv_sem=recv,
            device_id={"dp": along(axis, by)}, device_id_type=MESH,
        )

    def slot(job, m, by=0):
        return pl.ds(pl.multiple_of(((here[AXES[job]] + by + 4) % 4 * 2 + m) * R, R), R)

    def spread(job, m, d):
        ref = left.at[job, :, slot(job, m)]
        return remote(ref, ref, ag_s.at[job, m, d], ag_r.at[job, m, d], AXES[job], 1 - 2 * d)

    def relay(job, m, d):
        by = 1 - 2 * d
        ref = left.at[job, pl.ds(d * 640, 640), slot(job, m, -by)]
        return remote(ref, ref, fw_s.at[job, m, d], fw_r.at[job, m, d], AXES[job], by)

    def forward(m):
        for job in range(3):
            for d in range(2):
                spread(job, m, d).wait_recv()
                relay(job, m, d).start()

    def turned(job, m, by):
        rows = pl.ds(pl.multiple_of(m * R, R), R)
        return remote(
            stage.at[job, (here[AXES[job]] + by) % 4, rows], right.at[job, slot(job, m)],
            aa_s.at[job, m, by - 1], aa_r.at[job, m, by - 1], AXES[job], by,
        )

    def swap(job, m):
        rows = pl.ds(pl.multiple_of(m * R, R), R)
        value = (dpre, tot, dk)[job]
        for q in range(4):
            stage[job, q, rows, :Q] = value[rows, q * Q : (q + 1) * Q]
            stage[job, q, rows, Q:] = jnp.zeros((R, WIDE - Q), BF16)
        for by in (1, 3, 2):
            turned(job, m, by).start()
        right[job, slot(job, m), :] = stage[job, here[AXES[job]], rows, :]

    def sums(job, half, msg):
        by = 1 - 2 * half
        axis = 1 - AXES[job]
        pos = here[axis]
        o = pl.ds(2 * half, 2)
        sems = (js_s.at[job, half, msg], js_r.at[job, half, msg])
        if msg == 0:
            return remote(part.at[job, o, (pos + 2) % 4], p1.at[job, o], *sems, axis, by)
        if msg == 1:
            return remote(p1.at[job, o], p2.at[job, o], *sems, axis, by)
        return remote(part.at[job, o, (pos - by + 4) % 4], p3.at[job, o], *sems, axis, -by)

    def block_product(job):
        source = 2 - 2 * (s // 2) if job == 2 else job
        whole = jnp.dot(left[job], right[source], preferred_element_type=F32).astype(BF16)
        for j in range(16):
            at = (j // 4, j % 4) if AXES[job] == 0 else (j % 4, j // 4)
            part[job, *at] = whole[j * 80 : (j + 1) * 80]

        for half in range(2):
            sums(job, half, 0).start()
            sums(job, half, 2).start()

    def pair(k):
        return pltpu.make_async_remote_copy(
            src_ref=hs.at[k, 1 - xh], dst_ref=hr.at[k], send_sem=xh_s.at[k], recv_sem=xh_r.at[k],
            device_id={"dp": partner}, device_id_type=MESH,
        )

    def last(job, by):
        return remote(
            fs.at[job, (here[AXES[job]] + by) % 4], fr.at[job, here[AXES[job]]],
            fin_s.at[job, by - 1], fin_r.at[job, by - 1], AXES[job], by,
        )

    def turn_weights():
        @pl.loop(0, C // TILE)
        def _(j):
            span = pl.ds(pl.multiple_of(j * TILE, TILE), TILE)
            for k, w in enumerate((w1, w2, w3)):
                for n in columns:
                    wt[k, n, span] = w[span, n].T

    @pl.loop(0, 4)
    def _(i):
        kind = on3 * (i % 2) + (1 - on3) * (i // 2)
        m = on3 * (i // 2) + (1 - on3) * (i % 2)
        rows = pl.ds(pl.multiple_of(m * R, R), R)

        @pl.when((i == 0) & (s >= 2))
        def _():
            for n in (0, 2, 3):
                loads[n].wait()
            turn_weights()

        @pl.when(kind == 0)
        def _():
            @pl.when((s == 0) & (m == 0))
            def _():
                x_load.wait()

            @pl.when(s > 0)
            def _():
                send_x(m).wait_recv()

            @pl.when((i == 0) & (s < 2))
            def _():
                loads[0].wait()

            for n in columns:
                pre[rows, n] = jnp.dot(x[rows, :], w1[:, n], preferred_element_type=F32)

            @pl.when(i == 0)
            def _():
                loads[1].wait()
                row = lax.broadcasted_iota(jnp.int32, (8, table.shape[0]), 0)
                chosen = jnp.where(row == 0, steps[0], steps[1])
                hot = lax.broadcasted_iota(jnp.int32, (8, table.shape[0]), 1) == chosen
                found = jnp.dot(hot.astype(F32).astype(BF16), rows_t[...], preferred_element_type=F32)
                bias[0] = found[0:1]
                bias[1] = found[1:2]

                @pl.when(s < 2)
                def _():
                    loads[2].wait()
                    loads[3].wait()

            @pl.when(s >= 2)
            def _():
                send_sk(m).wait_recv()
                for n in columns:
                    pre[rows, n] += jnp.dot(sk[rows, :], w3[:, n], preferred_element_type=F32)

            for n in columns:
                v = pre[rows, n] + bias[m, :, n]
                g = 1.0 / (1.0 + jnp.exp(-v))
                gat[rows, n] = (v * g).astype(BF16)
                pre[rows, n] = g * (1.0 + v * (1.0 - g))
            for n in columns:
                po[rows, n] = (
                    x[rows, n].astype(F32)
                    + jnp.dot(gat[rows, :], w2[:, n], preferred_element_type=F32)
                ).astype(BF16)

            @pl.when(i == 0)
            def _():
                pl.semaphore_wait(barrier, 10)

            @pl.when(s < 3)
            def _():
                send_x(m).start()

            @pl.when(s < 2)
            def _():
                for n in columns:
                    sk[rows, n] = jnp.dot(
                        po[rows, :], w3[:, n], preferred_element_type=F32
                    ).astype(BF16)

                @pl.when(s == 1)
                def _():
                    send_sk(m).start()

                    @pl.when(m == 1)
                    def _():
                        for j in range(2):
                            send_x(j).wait_send()
                            send_sk(j).wait_send()
                        pl.semaphore_signal(turn, inc=1, device_id={"segment": 0}, device_id_type=MESH)

                @pl.when(s == 0)
                def _():
                    @pl.when(m == 1)
                    def _():
                        pl.semaphore_wait(turn, 1)

                    send_sk(m).start()

        @pl.when(kind == 1)
        def _():
            @pl.when((s == 3) & (m == 0))
            def _():
                up_load.wait()

            @pl.when(s < 2)
            def _():
                send_dk(m).wait_recv()
                swap(2, m)
                for n in columns:
                    acc[:, n] = jnp.dot(dk[rows, :], wt[2, :, n], preferred_element_type=F32)

            @pl.when(s < 3)
            def _():
                send_up(m).wait_recv()

            @pl.when(s < 2)
            def _():
                tot[rows, :] = (up[rows, :].astype(F32) + acc[...]).astype(BF16)

            @pl.when(s >= 2)
            def _():
                tot[rows, :] = up[rows, :]

            for n in columns:
                dpre[rows, n] = (
                    jnp.dot(tot[rows, :], wt[1, :, n], preferred_element_type=F32)
                    * pre[rows, n]
                ).astype(BF16)

            @pl.when(s == 0)
            def _():
                swap(1, m)
                swap(0, m)

            @pl.when(s == 2)
            def _():
                for n in columns:
                    dk[rows, n] = jnp.dot(
                        dpre[rows, :], wt[2, :, n], preferred_element_type=F32
                    ).astype(BF16)
                send_dk(m).start()

            for n in columns:
                gi[rows, n] = (
                    tot[rows, n].astype(F32)
                    + jnp.dot(dpre[rows, :], wt[0, :, n], preferred_element_type=F32)
                ).astype(BF16)

            @pl.when(s > 0)
            def _():
                send_up(m).start()

            @pl.when(s == 3)
            def _():
                for n in columns:
                    dk[rows, n] = jnp.dot(
                        dpre[rows, :], wt[2, :, n], preferred_element_type=F32
                    ).astype(BF16)
                send_dk(m).start()

            @pl.when(s > 0)
            def _():
                swap(1, m)
                swap(0, m)

        @pl.when(kind == on3)
        def _():
            for n in columns:
                left[0, n, slot(0, m)] = x[rows, n].T
                left[1, n, slot(1, m)] = gat[rows, n].T

            @pl.when(s < 2)
            def _():
                for n in columns:
                    left[2, n, slot(2, m)] = po[rows, n].T

            @pl.when(s >= 2)
            def _():
                for n in columns:
                    left[2, n, slot(2, m)] = sk[rows, n].T

            for job in range(3):
                for d in range(2):
                    spread(job, m, d).start()

        @pl.when((i == 1) & (s < 2))
        def _():
            forward(0)
            turn_weights()
            forward(1)

    @pl.when(s >= 2)
    def _():
        forward(0)
        forward(1)

    def gathered(job):
        for m in range(2):
            for d in range(2):
                relay(job, m, d).wait_recv()

    def arrived(job):
        for m in range(2):
            for by in (1, 2, 3):
                turned(job, m, by).wait_recv()

    def passed(job):
        for half in range(2):
            o = pl.ds(2 * half, 2)
            sums(job, half, 0).wait_recv()
            pos = (here[1 - AXES[job]] + 5 - 2 * half) % 4
            p1[job, o] = (p1[job, o].astype(F32) + part[job, o, pos].astype(F32)).astype(BF16)
            sums(job, half, 1).start()

    gathered(2)

    @pl.when(s < 2)
    def _():
        arrived(2)

    @pl.when(s >= 2)
    def _():
        arrived(0)

    block_product(2)
    gathered(1)
    arrived(1)
    block_product(1)
    passed(2)
    gathered(0)

    @pl.when(s < 2)
    def _():
        arrived(0)

    block_product(0)
    passed(1)
    passed(0)
    for job in (2, 1, 0):
        for half in range(2):
            sums(job, half, 1).wait_recv()
            sums(job, half, 2).wait_recv()
            for o in (2 * half, 2 * half + 1):
                total = (
                    part[job, o, here[1 - AXES[job]]].astype(F32)
                    + p2[job, o].astype(F32)
                    + p3[job, o].astype(F32)
                )
                hs[job, 0, o] = total[:40].astype(BF16)
                hs[job, 1, o] = total[40:].astype(BF16)
        pair(job).start()
    for job in (2, 1, 0):
        pair(job).wait_recv()
        for o in range(4):
            fs[job, o] = (hs[job, xh, o].astype(F32) + hr[job, o].astype(F32)).astype(BF16)
        for by in (1, 3, 2):
            last(job, by).start()
        fr[job, here[AXES[job]]] = fs[job, here[AXES[job]]]
    for job in (2, 1, 0):
        for by in (1, 2, 3):
            last(job, by).wait_recv()
        for q in range(4):
            (g_in, g_out, g_skip)[job][:, q * Q : (q + 1) * Q] = fr[job, q, :, :Q].astype(F32)
    for job in range(3):
        pair(job).wait_send()
        for n in range(3):
            last(job, n + 1).wait_send()
        for m in range(2):
            for n in range(3):
                sums(job, m, n).wait_send()
                if job < 2:
                    turned(job, m, n + 1).wait_send()
            for d in range(2):
                spread(job, m, d).wait_send()
                relay(job, m, d).wait_send()

    @pl.when(s < 2)
    def _():
        for m in range(2):
            for n in range(3):
                turned(2, m, n + 1).wait_send()

    for m in range(2):

        @pl.when((s == 0) | (s == 2))
        def _():
            send_x(m).wait_send()

        @pl.when(s == 0)
        def _():
            send_sk(m).wait_send()

        @pl.when(s > 0)
        def _():
            send_up(m).wait_send()

        @pl.when(s >= 2)
        def _():
            send_dk(m).wait_send()


def deliver(*refs):
    sem = refs[-1]
    copies = [pltpu.make_async_copy(refs[n], refs[5 + n], sem.at[n]) for n in range(5)]
    for copy in copies:
        copy.start()
    for copy in copies:
        copy.wait()


def body(latents, cotangent, timesteps, time_table, w_in, w_out, w_skip):
    rows = 2 * R
    vmem = pl.BlockSpec(memory_space=pltpu.VMEM)
    hbm = pl.BlockSpec(memory_space=pltpu.HBM)
    act = pltpu.VMEM((rows, C), BF16)
    weight = pltpu.VMEM((C, C), BF16)
    sums = pltpu.VMEM((3, 4, 80, WIDE), BF16)
    halves = pltpu.VMEM((3, 4, 40, WIDE), BF16)
    dma = pltpu.SemaphoreType.DMA
    out_act = jax.ShapeDtypeStruct((rows, C), BF16)
    out_grad = jax.ShapeDtypeStruct((40, C), F32)
    outs = (out_act, out_act, out_grad, out_grad, out_grad)
    results = pl.pallas_call(
        kernel,
        name="window",
        out_shape=outs,
        in_specs=[hbm, hbm, pl.BlockSpec(memory_space=pltpu.SMEM), hbm, hbm, hbm, hbm],
        out_specs=[vmem] * 5,
        scratch_shapes=[
            weight, weight, weight,
            pltpu.VMEM((3, C, C), BF16),
            pltpu.VMEM((1000, C), BF16),
            pltpu.VMEM((2, 1, C), F32),
            pltpu.VMEM((R, C), F32),
            act, act, act, act,
            pltpu.VMEM((rows, C), F32),
            act, act, act,
            pltpu.VMEM((3, C, 4 * rows), BF16),
            pltpu.VMEM((3, 4, rows, WIDE), BF16),
            pltpu.VMEM((3, 4 * rows, WIDE), BF16),
            pltpu.VMEM((3, 4, 4, 80, WIDE), BF16),
            sums, sums, sums,
            pltpu.VMEM((3, 2, 4, 40, WIDE), BF16),
            halves, halves, halves,
            dma((4,)),
            pltpu.SemaphoreType.REGULAR,
            dma((2,)), dma((3,)),
            dma((2,)), dma((2,)),
            dma((2,)), dma((3,)),
            dma((2,)), dma((2,)),
            dma((3,)), dma((3,)),
            dma((3, 2, 2)), dma((3, 2, 2)),
            dma((3, 2, 2)), dma((3, 2, 2)),
            dma((3, 2, 3)), dma((3, 2, 3)),
            dma((3, 2, 3)), dma((3, 2, 3)),
            dma((3, 3)), dma((3, 3)),
        ],
        compiler_params=pltpu.CompilerParams(
            collective_id=0, has_side_effects=True, vmem_limit_bytes=54_000_000
        ),
    )(
        latents.reshape(rows, C), cotangent.reshape(rows, C), timesteps.reshape(2), time_table.reshape(1000, C),
        w_in.reshape(C, C), w_out.reshape(C, C), w_skip.reshape(C, C),
    )
    po, gi, g_in, g_out, g_skip = pl.pallas_call(
        deliver,
        name="deliver",
        out_shape=outs,
        in_specs=[vmem] * 5,
        out_specs=[hbm] * 5,
        scratch_shapes=[dma((5,))],
        compiler_params=pltpu.CompilerParams(vmem_limit_bytes=4_000_000),
    )(*results)
    return (
        po.reshape(1, 2, R, C),
        gi.reshape(1, 2, R, C),
        g_in[None],
        g_out[None],
        g_skip[None],
    )


def solution(mesh):
    in_specs = (
        P(None, "dp", None),
        P(None, "dp", None),
        P(None, "dp"),
        P("segment", None, None),
        P("segment", None, None),
        P("segment", None, None),
        P("segment", None, None),
    )
    out_specs = (
        P("segment", None, "dp", None),
        P("segment", None, "dp", None),
        P("segment", "dp", None),
        P("segment", "dp", None),
        P("segment", "dp", None),
    )
    return jax.shard_map(body, mesh=mesh, in_specs=in_specs, out_specs=out_specs, check_vma=False)
```

```python
import jax
import jax.numpy as jnp
from jax import lax
from jax.experimental import pallas as pl
from jax.experimental.pallas import tpu as pltpu
from jax.sharding import PartitionSpec as P

MESH = pl.DeviceIdType.MESH
F32 = jnp.float32
BF16 = jnp.bfloat16
C = 1280
R = 128
TILE = 256
BLOCKS = ((0, 0, 384, 0, 1), (1, 384, 256, 0, -1), (2, 640, 256, 1, 1), (3, 896, 384, 1, -1))
Q = C // 4
WIDE = 384


def kernel(
    lat, cot, steps, table, w_in, w_out, w_skip,
    po, gi, g_in, g_out, g_skip,
    w1, w2, w3, wt, rows_t, bias, acc, x, up, sk, dk, pre, gat, tot, dpre, lt, grads, r1, r2, r3, s1, q1, q2, q3, xs, xr,
    left, stage, right, part, p1, p2, p3, hs, hr, fs, fr,
    wsem, turn, x_s, x_r, sk_s, sk_r, up_s, up_r, dk_s, dk_r, rs_s, rs_r, xh_s, xh_r,
    ag_s, ag_r, fw_s, fw_r, aa_s, aa_r, js_s, js_r, fin_s, fin_r,
):
    s = lax.axis_index("segment")
    dp = lax.axis_index("dp")
    z = dp // 8
    y = (dp // 2) % 4
    xh = dp % 2

    def along(axis, by):
        if axis == 0:
            return ((z + by + 4) % 4) * 8 + y * 2 + xh
        return z * 8 + ((y + by + 4) % 4) * 2 + xh

    partner = z * 8 + y * 2 + (1 - xh)
    loads = [
        pltpu.make_async_copy(src, dst, wsem.at[n])
        for n, (src, dst) in enumerate(((w_in, w1), (table, rows_t), (w_out, w2), (w_skip, w3)))
    ]
    x_load = pltpu.make_async_copy(lat, x, x_r.at[2])
    up_load = pltpu.make_async_copy(cot, up, up_r.at[2])

    @pl.when(s == 0)
    def _():
        x_load.start()

    for load in loads:
        load.start()

    @pl.when(s == 3)
    def _():
        up_load.start()

    barrier = pltpu.get_barrier_semaphore()
    for by in (1, 2, 3):
        pl.semaphore_signal(barrier, inc=1, device_id={"segment": (s + by) % 4}, device_id_type=MESH)
    for other in [along(axis, by) for axis in (0, 1) for by in (1, 2, 3)] + [partner]:
        pl.semaphore_signal(barrier, inc=1, device_id={"dp": other}, device_id_type=MESH)

    def hand(buf, dst, m, send, recv, to):
        rows = pl.ds(pl.multiple_of(m * R, R), R)
        return pltpu.make_async_remote_copy(
            src_ref=buf.at[rows], dst_ref=dst.at[rows], send_sem=send.at[m], recv_sem=recv.at[m],
            device_id={"segment": to}, device_id_type=MESH,
        )

    def send_x(m):
        return hand(po, x, m, x_s, x_r, (s + 1) % 4)

    def send_sk(m):
        return hand(sk, sk, m, sk_s, sk_r, 3 - s)

    def send_up(m):
        return hand(gi, up, m, up_s, up_r, (s + 3) % 4)

    def send_dk(m):
        return hand(dk, dk, m, dk_s, dk_r, 3 - s)

    columns = [pl.ds(n * TILE, TILE) for n in range(C // TILE)]
    on3 = s // 3

    here = (z, y)

    def ring(step, msg, block, src, dst, axis, by):
        n = block[0]
        return pltpu.make_async_remote_copy(
            src_ref=src, dst_ref=dst, send_sem=rs_s.at[step, msg, n], recv_sem=rs_r.at[step, msg, n],
            device_id={"dp": along(axis, by)}, device_id_type=MESH,
        )

    def piece(block, pos):
        _, col, width, colour, _ = block
        cols = pl.ds(col, width)
        if colour == 0:
            return grads.at[pos % 4, :, :, cols]
        return grads.at[:, pos % 4, :, cols]

    def first(block, msg):
        _, col, width, colour, by = block
        cols = pl.ds(col, width)
        pos = here[colour]
        if msg == 0:
            return ring(0, 0, block, piece(block, pos + 2), r1.at[:, :, cols], colour, by)
        if msg == 1:
            return ring(0, 1, block, r1.at[:, :, cols], r2.at[:, :, cols], colour, by)
        return ring(0, 2, block, piece(block, pos - by + 4), r3.at[:, :, cols], colour, -by)

    def second(block, msg):
        _, col, width, colour, by = block
        cols = pl.ds(col, width)
        axis = 1 - colour
        pos = here[axis]
        if msg == 0:
            return ring(1, 0, block, s1.at[(pos + 2) % 4, :, cols], q1.at[:, cols], axis, by)
        if msg == 1:
            return ring(1, 1, block, q1.at[:, cols], q2.at[:, cols], axis, by)
        return ring(1, 2, block, s1.at[(pos - by + 4) % 4, :, cols], q3.at[:, cols], axis, -by)

    def product(other):
        for n in columns:
            whole = jnp.dot(lt[...], other[:, n], preferred_element_type=F32).astype(BF16)
            for j in range(16):
                grads[j // 4, j % 4, :, n] = whole[j * 80 : (j + 1) * 80]

        for block in BLOCKS:
            first(block, 0).start()
            first(block, 2).start()

    def remote(src, dst, send, recv, axis, by):
        return pltpu.make_async_remote_copy(
            src_ref=src, dst_ref=dst, send_sem=send, recv_sem=recv,
            device_id={"dp": along(axis, by)}, device_id_type=MESH,
        )

    def slot(job, m, by=0):
        return pl.ds(pl.multiple_of(((here[job] + by + 4) % 4 * 2 + m) * R, R), R)

    def spread(job, m, d):
        ref = left.at[job, :, slot(job, m)]
        return remote(ref, ref, ag_s.at[job, m, d], ag_r.at[job, m, d], job, 1 - 2 * d)

    def relay(job, m, d):
        by = 1 - 2 * d
        ref = left.at[job, pl.ds(d * 640, 640), slot(job, m, -by)]
        return remote(ref, ref, fw_s.at[job, m, d], fw_r.at[job, m, d], job, by)

    def forward(m):
        for job in range(2):
            for d in range(2):
                spread(job, m, d).wait_recv()
                relay(job, m, d).start()

    def turned(job, m, by):
        rows = pl.ds(pl.multiple_of(m * R, R), R)
        return remote(
            stage.at[job, (here[job] + by) % 4, rows], right.at[job, slot(job, m)],
            aa_s.at[job, m, by - 1], aa_r.at[job, m, by - 1], job, by,
        )

    def swap(job, m):
        rows = pl.ds(pl.multiple_of(m * R, R), R)
        value = (dpre, tot)[job]
        for q in range(4):
            stage[job, q, rows, :Q] = value[rows, q * Q : (q + 1) * Q]
            stage[job, q, rows, Q:] = jnp.zeros((R, WIDE - Q), BF16)
        for by in (1, 3, 2):
            turned(job, m, by).start()
        right[job, slot(job, m), :] = stage[job, here[job], rows, :]

    def sums(job, half, msg):
        by = 1 - 2 * half
        axis = 1 - job
        pos = here[axis]
        o = pl.ds(2 * half, 2)
        sems = (js_s.at[job, half, msg], js_r.at[job, half, msg])
        if msg == 0:
            return remote(part.at[job, o, (pos + 2) % 4], p1.at[job, o], *sems, axis, by)
        if msg == 1:
            return remote(p1.at[job, o], p2.at[job, o], *sems, axis, by)
        return remote(part.at[job, o, (pos - by + 4) % 4], p3.at[job, o], *sems, axis, -by)

    def block_product(job):
        whole = jnp.dot(left[job], right[job], preferred_element_type=F32).astype(BF16)
        for j in range(16):
            at = (j // 4, j % 4) if job == 0 else (j % 4, j // 4)
            part[job, *at, :, :Q] = whole[j * 80 : j * 80 + 40, :Q]
            part[job, *at, :, Q:] = whole[j * 80 + 40 : (j + 1) * 80, :Q]

        for half in range(2):
            sums(job, half, 0).start()
            sums(job, half, 2).start()

    def pair(k):
        src, dst = ((hs.at[0, 1 - xh], hr.at[0]), (hs.at[1, 1 - xh], hr.at[1]), (xs.at[1 - xh], xr))[k]
        return pltpu.make_async_remote_copy(
            src_ref=src, dst_ref=dst, send_sem=xh_s.at[k], recv_sem=xh_r.at[k],
            device_id={"dp": partner}, device_id_type=MESH,
        )

    def last(job, by):
        return remote(
            fs.at[job, (here[job] + by) % 4], fr.at[job, here[job]],
            fin_s.at[job, by - 1], fin_r.at[job, by - 1], job, by,
        )

    @pl.loop(0, 4)
    def _(i):
        kind = on3 * (i % 2) + (1 - on3) * (i // 2)
        m = on3 * (i // 2) + (1 - on3) * (i % 2)
        rows = pl.ds(pl.multiple_of(m * R, R), R)

        @pl.when((i == 0) & (s >= 2))
        def _():
            for n in (0, 2, 3):
                loads[n].wait()

        @pl.when(i == 2 * (1 - s // 2))
        def _():
            @pl.loop(0, C // TILE)
            def _(j):
                span = pl.ds(pl.multiple_of(j * TILE, TILE), TILE)
                for k, w in enumerate((w1, w2, w3)):
                    for n in columns:
                        wt[k, n, span] = w[span, n].T

        @pl.when(kind == 0)
        def _():
            @pl.when((s == 0) & (m == 0))
            def _():
                x_load.wait()

            @pl.when(s > 0)
            def _():
                send_x(m).wait_recv()

            @pl.when((i == 0) & (s < 2))
            def _():
                loads[0].wait()

            for n in columns:
                pre[rows, n] = jnp.dot(x[rows, :], w1[:, n], preferred_element_type=F32)

            @pl.when(i == 0)
            def _():
                loads[1].wait()
                row = lax.broadcasted_iota(jnp.int32, (8, table.shape[0]), 0)
                chosen = jnp.where(row == 0, steps[0], steps[1])
                hot = lax.broadcasted_iota(jnp.int32, (8, table.shape[0]), 1) == chosen
                found = jnp.dot(hot.astype(F32).astype(BF16), rows_t[...], preferred_element_type=F32)
                bias[0] = found[0:1]
                bias[1] = found[1:2]

                @pl.when(s < 2)
                def _():
                    loads[2].wait()
                    loads[3].wait()

            @pl.when(s >= 2)
            def _():
                send_sk(m).wait_recv()
                for n in columns:
                    pre[rows, n] += jnp.dot(sk[rows, :], w3[:, n], preferred_element_type=F32)

            for n in columns:
                v = pre[rows, n] + bias[m, :, n]
                g = 1.0 / (1.0 + jnp.exp(-v))
                gat[rows, n] = (v * g).astype(BF16)
                pre[rows, n] = g * (1.0 + v * (1.0 - g))
            for n in columns:
                po[rows, n] = (
                    x[rows, n].astype(F32)
                    + jnp.dot(gat[rows, :], w2[:, n], preferred_element_type=F32)
                ).astype(BF16)

            @pl.when(i == 0)
            def _():
                pl.semaphore_wait(barrier, 10)

            @pl.when(s < 3)
            def _():
                send_x(m).start()

            @pl.when(s < 2)
            def _():
                for n in columns:
                    sk[rows, n] = jnp.dot(
                        po[rows, :], w3[:, n], preferred_element_type=F32
                    ).astype(BF16)

                @pl.when(s == 1)
                def _():
                    send_sk(m).start()

                    @pl.when(m == 1)
                    def _():
                        for j in range(2):
                            send_x(j).wait_send()
                            send_sk(j).wait_send()
                        pl.semaphore_signal(turn, inc=1, device_id={"segment": 0}, device_id_type=MESH)

                @pl.when(s == 0)
                def _():
                    @pl.when(m == 1)
                    def _():
                        pl.semaphore_wait(turn, 1)

                    send_sk(m).start()

        @pl.when(kind == 1)
        def _():
            @pl.when((s == 3) & (m == 0))
            def _():
                up_load.wait()

            @pl.when(s < 2)
            def _():
                send_dk(m).wait_recv()
                for n in columns:
                    acc[:, n] = jnp.dot(dk[rows, :], wt[2, :, n], preferred_element_type=F32)

                @pl.when((m == 1) & (s < 2))
                def _():
                    product(dk)

            @pl.when(s < 3)
            def _():
                send_up(m).wait_recv()

            @pl.when(s < 2)
            def _():
                tot[rows, :] = (up[rows, :].astype(F32) + acc[...]).astype(BF16)

            @pl.when(s >= 2)
            def _():
                tot[rows, :] = up[rows, :]

            for n in columns:
                dpre[rows, n] = (
                    jnp.dot(tot[rows, :], wt[1, :, n], preferred_element_type=F32)
                    * pre[rows, n]
                ).astype(BF16)

            @pl.when(s == 0)
            def _():
                swap(1, m)
                swap(0, m)

            @pl.when(s == 2)
            def _():
                for n in columns:
                    dk[rows, n] = jnp.dot(
                        dpre[rows, :], wt[2, :, n], preferred_element_type=F32
                    ).astype(BF16)
                send_dk(m).start()

            for n in columns:
                gi[rows, n] = (
                    tot[rows, n].astype(F32)
                    + jnp.dot(dpre[rows, :], wt[0, :, n], preferred_element_type=F32)
                ).astype(BF16)

            @pl.when(s > 0)
            def _():
                send_up(m).start()

            @pl.when(s == 3)
            def _():
                for n in columns:
                    dk[rows, n] = jnp.dot(
                        dpre[rows, :], wt[2, :, n], preferred_element_type=F32
                    ).astype(BF16)
                send_dk(m).start()

            @pl.when(s > 0)
            def _():
                swap(1, m)
                swap(0, m)

        @pl.when(kind == on3)
        def _():
            for n in columns:
                left[0, n, slot(0, m)] = x[rows, n].T
                left[1, n, slot(1, m)] = gat[rows, n].T
            for job in range(2):
                for d in range(2):
                    spread(job, m, d).start()

            @pl.when(s < 2)
            def _():
                for n in columns:
                    lt[n, rows] = po[rows, n].T

            @pl.when(s >= 2)
            def _():
                for n in columns:
                    lt[n, rows] = sk[rows, n].T

        @pl.when(i == 1 + 2 * on3)
        def _():
            forward(0)

        @pl.when(((i == 1) & (s < 2)) | ((i == 2) & (s == 2)))
        def _():
            forward(1)

    @pl.when(s == 3)
    def _():
        forward(1)

    @pl.when(s >= 2)
    def _():
        product(dpre)

    def gathered(job):
        for m in range(2):
            for d in range(2):
                relay(job, m, d).wait_recv()
            for by in (1, 2, 3):
                turned(job, m, by).wait_recv()

    for block in BLOCKS:
        _, col, width, colour, by = block
        cols = pl.ds(col, width)
        first(block, 0).wait_recv()
        r1[:, :, cols] = (
            r1[:, :, cols].astype(F32) + piece(block, here[colour] + by + 4)[...].astype(F32)
        ).astype(BF16)
        first(block, 1).start()
    gathered(1)
    block_product(1)
    gathered(0)
    block_product(0)
    for job in (1, 0):
        for half in range(2):
            o = pl.ds(2 * half, 2)
            sums(job, half, 0).wait_recv()
            pos = (here[1 - job] + 5 - 2 * half) % 4
            p1[job, o] = (p1[job, o].astype(F32) + part[job, o, pos].astype(F32)).astype(BF16)
            sums(job, half, 1).start()
    for job in (1, 0):
        for half in range(2):
            sums(job, half, 1).wait_recv()
            sums(job, half, 2).wait_recv()
            for o in (2 * half, 2 * half + 1):
                total = (
                    part[job, o, here[1 - job]].astype(F32)
                    + p2[job, o].astype(F32)
                    + p3[job, o].astype(F32)
                )
                lanes = pl.ds(o % 2 * Q, Q)
                hs[job, 0, half, :, lanes] = total[:, :Q].astype(BF16)
                hs[job, 1, half, :, lanes] = total[:, Q:].astype(BF16)
        pair(job).start()
    for block in BLOCKS:
        _, col, width, colour, by = block
        cols = pl.ds(col, width)
        first(block, 1).wait_recv()
        first(block, 2).wait_recv()
        s1[:, :, cols] = (
            piece(block, here[colour])[...].astype(F32)
            + r2[:, :, cols].astype(F32)
            + r3[:, :, cols].astype(F32)
        ).astype(BF16)
        second(block, 0).start()
        second(block, 2).start()
    for block in BLOCKS:
        _, col, width, colour, by = block
        cols = pl.ds(col, width)
        second(block, 0).wait_recv()
        pos = (here[1 - colour] + by + 4) % 4
        q1[:, cols] = (q1[:, cols].astype(F32) + s1[pos, :, cols].astype(F32)).astype(BF16)
        second(block, 1).start()
    for job in (1, 0):
        pair(job).wait_recv()
        for o in range(4):
            lanes = pl.ds(o % 2 * Q, Q)
            mine = hs[job, xh, o // 2, :, lanes].astype(F32)
            fs[job, o, :, :Q] = (mine + hr[job, o // 2, :, lanes].astype(F32)).astype(BF16)
            fs[job, o, :, Q:] = jnp.zeros((40, WIDE - Q), BF16)
        for by in (1, 3, 2):
            last(job, by).start()
        fr[job, here[job]] = fs[job, here[job]]
    for block in BLOCKS:
        _, col, width, colour, by = block
        cols = pl.ds(col, width)
        second(block, 1).wait_recv()
        second(block, 2).wait_recv()
        total = (
            s1[here[1 - colour], :, cols].astype(F32)
            + q2[:, cols].astype(F32)
            + q3[:, cols].astype(F32)
        )
        xs[0, :, cols] = total[:40].astype(BF16)
        xs[1, :, cols] = total[40:].astype(BF16)
    pair(2).start()
    for job in (1, 0):
        for by in (1, 2, 3):
            last(job, by).wait_recv()
        for q in range(4):
            (g_in, g_out)[job][:, q * Q : (q + 1) * Q] = fr[job, q, :, :Q].astype(F32)
    pair(2).wait_recv()
    g_skip[...] = xs[xh].astype(F32) + xr[...].astype(F32)
    for block in BLOCKS:
        for msg in range(3):
            first(block, msg).wait_send()
            second(block, msg).wait_send()
    for k in range(3):
        pair(k).wait_send()
    for job in range(2):
        for n in range(3):
            last(job, n + 1).wait_send()
            for m in range(2):
                turned(job, m, n + 1).wait_send()
                sums(job, m, n).wait_send()
        for m in range(2):
            for d in range(2):
                spread(job, m, d).wait_send()
                relay(job, m, d).wait_send()
    for m in range(2):

        @pl.when((s == 0) | (s == 2))
        def _():
            send_x(m).wait_send()

        @pl.when(s == 0)
        def _():
            send_sk(m).wait_send()

        @pl.when(s > 0)
        def _():
            send_up(m).wait_send()

        @pl.when(s >= 2)
        def _():
            send_dk(m).wait_send()


def deliver(*refs):
    sem = refs[-1]
    copies = [pltpu.make_async_copy(refs[n], refs[5 + n], sem.at[n]) for n in range(5)]
    for copy in copies:
        copy.start()
    for copy in copies:
        copy.wait()


def body(latents, cotangent, timesteps, time_table, w_in, w_out, w_skip):
    rows = 2 * R
    vmem = pl.BlockSpec(memory_space=pltpu.VMEM)
    hbm = pl.BlockSpec(memory_space=pltpu.HBM)
    act = pltpu.VMEM((rows, C), BF16)
    weight = pltpu.VMEM((C, C), BF16)
    quarter = pltpu.VMEM((4, 80, C), BF16)
    sixteenth = pltpu.VMEM((80, C), BF16)
    sums = pltpu.VMEM((2, 4, 40, 2 * Q), BF16)
    halves = pltpu.VMEM((2, 4, 40, WIDE), BF16)
    dma = pltpu.SemaphoreType.DMA
    out_act = jax.ShapeDtypeStruct((rows, C), BF16)
    out_grad = jax.ShapeDtypeStruct((40, C), F32)
    outs = (out_act, out_act, out_grad, out_grad, out_grad)
    results = pl.pallas_call(
        kernel,
        name="window",
        out_shape=outs,
        in_specs=[hbm, hbm, pl.BlockSpec(memory_space=pltpu.SMEM), hbm, hbm, hbm, hbm],
        out_specs=[vmem] * 5,
        scratch_shapes=[
            weight, weight, weight,
            pltpu.VMEM((3, C, C), BF16),
            pltpu.VMEM((1000, C), BF16),
            pltpu.VMEM((2, 1, C), F32),
            pltpu.VMEM((R, C), F32),
            act, act, act, act,
            pltpu.VMEM((rows, C), F32),
            act, act, act,
            pltpu.VMEM((C, rows), BF16),
            pltpu.VMEM((4, 4, 80, C), BF16),
            quarter, quarter, quarter, quarter,
            sixteenth, sixteenth, sixteenth,
            pltpu.VMEM((2, 40, C), BF16),
            pltpu.VMEM((40, C), BF16),
            pltpu.VMEM((2, C, 4 * rows), BF16),
            pltpu.VMEM((2, 4, rows, WIDE), BF16),
            pltpu.VMEM((2, 4 * rows, WIDE), BF16),
            pltpu.VMEM((2, 4, 4, 40, 2 * Q), BF16),
            sums, sums, sums,
            pltpu.VMEM((2, 2, 2, 40, 2 * Q), BF16),
            pltpu.VMEM((2, 2, 40, 2 * Q), BF16),
            halves, halves,
            dma((4,)),
            pltpu.SemaphoreType.REGULAR,
            dma((2,)), dma((3,)),
            dma((2,)), dma((2,)),
            dma((2,)), dma((3,)),
            dma((2,)), dma((2,)),
            dma((2, 3, 4)), dma((2, 3, 4)),
            dma((3,)), dma((3,)),
            dma((2, 2, 2)), dma((2, 2, 2)),
            dma((2, 2, 2)), dma((2, 2, 2)),
            dma((2, 2, 3)), dma((2, 2, 3)),
            dma((2, 2, 3)), dma((2, 2, 3)),
            dma((2, 3)), dma((2, 3)),
        ],
        compiler_params=pltpu.CompilerParams(
            collective_id=0, has_side_effects=True, vmem_limit_bytes=54_000_000
        ),
    )(
        latents.reshape(rows, C), cotangent.reshape(rows, C), timesteps.reshape(2), time_table.reshape(1000, C),
        w_in.reshape(C, C), w_out.reshape(C, C), w_skip.reshape(C, C),
    )
    po, gi, g_in, g_out, g_skip = pl.pallas_call(
        deliver,
        name="deliver",
        out_shape=outs,
        in_specs=[vmem] * 5,
        out_specs=[hbm] * 5,
        scratch_shapes=[dma((5,))],
        compiler_params=pltpu.CompilerParams(vmem_limit_bytes=4_000_000),
    )(*results)
    return (
        po.reshape(1, 2, R, C),
        gi.reshape(1, 2, R, C),
        g_in[None],
        g_out[None],
        g_skip[None],
    )


def solution(mesh):
    in_specs = (
        P(None, "dp", None),
        P(None, "dp", None),
        P(None, "dp"),
        P("segment", None, None),
        P("segment", None, None),
        P("segment", None, None),
        P("segment", None, None),
    )
    out_specs = (
        P("segment", None, "dp", None),
        P("segment", None, "dp", None),
        P("segment", "dp", None),
        P("segment", "dp", None),
        P("segment", "dp", None),
    )
    return jax.shard_map(body, mesh=mesh, in_specs=in_specs, out_specs=out_specs, check_vma=False)
```

```python
import jax
import jax.numpy as jnp
from jax import lax
from jax.experimental import pallas as pl
from jax.experimental.pallas import tpu as pltpu
from jax.sharding import PartitionSpec as P

MESH = pl.DeviceIdType.MESH
F32 = jnp.float32
BF16 = jnp.bfloat16
C = 1280
R = 128
TILE = 256
BLOCKS = ((0, 0, 384, 0, 1), (1, 384, 256, 0, -1), (2, 640, 256, 1, 1), (3, 896, 384, 1, -1))
Q = C // 4
WIDE = 384


def kernel(
    lat, cot, steps, table, w_in, w_out, w_skip,
    po, gi, g_in, g_out, g_skip,
    w1, w2, w3, wt, rows_t, bias, acc, x, up, sk, dk, pre, gat, tot, dpre, lt, grads, r1, r2, r3, s1, q1, q2, q3, xs, xr,
    left, stage, right, part, p1, p2, p3, hs, hr, fs, fr,
    wsem, turn, x_s, x_r, sk_s, sk_r, up_s, up_r, dk_s, dk_r, rs_s, rs_r, xh_s, xh_r,
    ag_s, ag_r, fw_s, fw_r, aa_s, aa_r, js_s, js_r, fin_s, fin_r,
):
    s = lax.axis_index("segment")
    dp = lax.axis_index("dp")
    z = dp // 8
    y = (dp // 2) % 4
    xh = dp % 2

    def along(axis, by):
        if axis == 0:
            return ((z + by + 4) % 4) * 8 + y * 2 + xh
        return z * 8 + ((y + by + 4) % 4) * 2 + xh

    partner = z * 8 + y * 2 + (1 - xh)
    loads = [
        pltpu.make_async_copy(src, dst, wsem.at[n])
        for n, (src, dst) in enumerate(((w_in, w1), (table, rows_t), (w_out, w2), (w_skip, w3)))
    ]
    x_load = pltpu.make_async_copy(lat, x, x_r.at[2])
    up_load = pltpu.make_async_copy(cot, up, up_r.at[2])

    @pl.when(s == 0)
    def _():
        x_load.start()

    for load in loads:
        load.start()

    @pl.when(s == 3)
    def _():
        up_load.start()

    barrier = pltpu.get_barrier_semaphore()
    for by in (1, 2, 3):
        pl.semaphore_signal(barrier, inc=1, device_id={"segment": (s + by) % 4}, device_id_type=MESH)
    for other in [along(axis, by) for axis in (0, 1) for by in (1, 2, 3)] + [partner]:
        pl.semaphore_signal(barrier, inc=1, device_id={"dp": other}, device_id_type=MESH)

    def hand(buf, dst, m, send, recv, to):
        rows = pl.ds(pl.multiple_of(m * R, R), R)
        return pltpu.make_async_remote_copy(
            src_ref=buf.at[rows], dst_ref=dst.at[rows], send_sem=send.at[m], recv_sem=recv.at[m],
            device_id={"segment": to}, device_id_type=MESH,
        )

    def send_x(m):
        return hand(po, x, m, x_s, x_r, (s + 1) % 4)

    def send_sk(m):
        return hand(sk, sk, m, sk_s, sk_r, 3 - s)

    def send_up(m):
        return hand(gi, up, m, up_s, up_r, (s + 3) % 4)

    def send_dk(m):
        return hand(dk, dk, m, dk_s, dk_r, 3 - s)

    columns = [pl.ds(n * TILE, TILE) for n in range(C // TILE)]
    on3 = s // 3

    here = (z, y)

    def ring(step, msg, block, src, dst, axis, by):
        n = block[0]
        return pltpu.make_async_remote_copy(
            src_ref=src, dst_ref=dst, send_sem=rs_s.at[step, msg, n], recv_sem=rs_r.at[step, msg, n],
            device_id={"dp": along(axis, by)}, device_id_type=MESH,
        )

    def piece(block, pos):
        _, col, width, colour, _ = block
        cols = pl.ds(col, width)
        if colour == 0:
            return grads.at[pos % 4, :, :, cols]
        return grads.at[:, pos % 4, :, cols]

    def first(block, msg):
        _, col, width, colour, by = block
        cols = pl.ds(col, width)
        pos = here[colour]
        if msg == 0:
            return ring(0, 0, block, piece(block, pos + 2), r1.at[:, :, cols], colour, by)
        if msg == 1:
            return ring(0, 1, block, r1.at[:, :, cols], r2.at[:, :, cols], colour, by)
        return ring(0, 2, block, piece(block, pos - by + 4), r3.at[:, :, cols], colour, -by)

    def second(block, msg):
        _, col, width, colour, by = block
        cols = pl.ds(col, width)
        axis = 1 - colour
        pos = here[axis]
        if msg == 0:
            return ring(1, 0, block, s1.at[(pos + 2) % 4, :, cols], q1.at[:, cols], axis, by)
        if msg == 1:
            return ring(1, 1, block, q1.at[:, cols], q2.at[:, cols], axis, by)
        return ring(1, 2, block, s1.at[(pos - by + 4) % 4, :, cols], q3.at[:, cols], axis, -by)

    def product(other):
        for n in columns:
            whole = jnp.dot(lt[...], other[:, n], preferred_element_type=F32).astype(BF16)
            for j in range(16):
                grads[j // 4, j % 4, :, n] = whole[j * 80 : (j + 1) * 80]

        for block in BLOCKS:
            first(block, 0).start()
            first(block, 2).start()

    def remote(src, dst, send, recv, axis, by):
        return pltpu.make_async_remote_copy(
            src_ref=src, dst_ref=dst, send_sem=send, recv_sem=recv,
            device_id={"dp": along(axis, by)}, device_id_type=MESH,
        )

    def slot(job, m, by=0):
        return pl.ds(pl.multiple_of(((here[job] + by + 4) % 4 * 2 + m) * R, R), R)

    def spread(job, m, d):
        ref = left.at[job, :, slot(job, m)]
        return remote(ref, ref, ag_s.at[job, m, d], ag_r.at[job, m, d], job, 1 - 2 * d)

    def relay(job, m, d):
        by = 1 - 2 * d
        ref = left.at[job, pl.ds(d * 640, 640), slot(job, m, -by)]
        return remote(ref, ref, fw_s.at[job, m, d], fw_r.at[job, m, d], job, by)

    def forward(m):
        for job in range(2):
            for d in range(2):
                spread(job, m, d).wait_recv()
                relay(job, m, d).start()

    def turned(job, m, by):
        rows = pl.ds(pl.multiple_of(m * R, R), R)
        return remote(
            stage.at[job, (here[job] + by) % 4, rows], right.at[job, slot(job, m)],
            aa_s.at[job, m, by - 1], aa_r.at[job, m, by - 1], job, by,
        )

    def swap(job, m):
        rows = pl.ds(pl.multiple_of(m * R, R), R)
        value = (dpre, tot)[job]
        for q in range(4):
            stage[job, q, rows, :Q] = value[rows, q * Q : (q + 1) * Q]
            stage[job, q, rows, Q:] = jnp.zeros((R, WIDE - Q), BF16)
        for by in (1, 3, 2):
            turned(job, m, by).start()
        right[job, slot(job, m), :] = stage[job, here[job], rows, :]

    def sums(job, half, msg):
        by = 1 - 2 * half
        axis = 1 - job
        pos = here[axis]
        o = pl.ds(2 * half, 2)
        sems = (js_s.at[job, half, msg], js_r.at[job, half, msg])
        if msg == 0:
            return remote(part.at[job, o, (pos + 2) % 4], p1.at[job, o], *sems, axis, by)
        if msg == 1:
            return remote(p1.at[job, o], p2.at[job, o], *sems, axis, by)
        return remote(part.at[job, o, (pos - by + 4) % 4], p3.at[job, o], *sems, axis, -by)

    def block_product(job):
        whole = jnp.dot(left[job], right[job], preferred_element_type=F32).astype(BF16)
        for j in range(16):
            at = (j // 4, j % 4) if job == 0 else (j % 4, j // 4)
            part[job, *at, :, :Q] = whole[j * 80 : j * 80 + 40, :Q]
            part[job, *at, :, Q:] = whole[j * 80 + 40 : (j + 1) * 80, :Q]

        for half in range(2):
            sums(job, half, 0).start()
            sums(job, half, 2).start()

    def pair(k):
        src, dst = ((hs.at[0, 1 - xh], hr.at[0]), (hs.at[1, 1 - xh], hr.at[1]), (xs.at[1 - xh], xr))[k]
        return pltpu.make_async_remote_copy(
            src_ref=src, dst_ref=dst, send_sem=xh_s.at[k], recv_sem=xh_r.at[k],
            device_id={"dp": partner}, device_id_type=MESH,
        )

    def last(job, by):
        return remote(
            fs.at[job, (here[job] + by) % 4], fr.at[job, here[job]],
            fin_s.at[job, by - 1], fin_r.at[job, by - 1], job, by,
        )

    @pl.loop(0, 4)
    def _(i):
        kind = on3 * (i % 2) + (1 - on3) * (i // 2)
        m = on3 * (i // 2) + (1 - on3) * (i % 2)
        rows = pl.ds(pl.multiple_of(m * R, R), R)

        @pl.when((i == 0) & (s >= 2))
        def _():
            for n in (0, 2, 3):
                loads[n].wait()

        @pl.when(i == 2 * (1 - s // 2))
        def _():
            @pl.loop(0, C // TILE)
            def _(j):
                span = pl.ds(pl.multiple_of(j * TILE, TILE), TILE)
                for k, w in enumerate((w1, w2, w3)):
                    for n in columns:
                        wt[k, n, span] = w[span, n].T

        @pl.when(kind == 0)
        def _():
            @pl.when((s == 0) & (m == 0))
            def _():
                x_load.wait()

            @pl.when(s > 0)
            def _():
                send_x(m).wait_recv()

            @pl.when((i == 0) & (s < 2))
            def _():
                loads[0].wait()

            for n in columns:
                pre[rows, n] = jnp.dot(x[rows, :], w1[:, n], preferred_element_type=F32)

            @pl.when(i == 0)
            def _():
                loads[1].wait()
                row = lax.broadcasted_iota(jnp.int32, (8, table.shape[0]), 0)
                chosen = jnp.where(row == 0, steps[0], steps[1])
                hot = lax.broadcasted_iota(jnp.int32, (8, table.shape[0]), 1) == chosen
                found = jnp.dot(hot.astype(F32).astype(BF16), rows_t[...], preferred_element_type=F32)
                bias[0] = found[0:1]
                bias[1] = found[1:2]

                @pl.when(s < 2)
                def _():
                    loads[2].wait()
                    loads[3].wait()

            @pl.when(s >= 2)
            def _():
                send_sk(m).wait_recv()
                for n in columns:
                    pre[rows, n] += jnp.dot(sk[rows, :], w3[:, n], preferred_element_type=F32)

            for n in columns:
                v = pre[rows, n] + bias[m, :, n]
                g = 1.0 / (1.0 + jnp.exp(-v))
                gat[rows, n] = (v * g).astype(BF16)
                pre[rows, n] = g * (1.0 + v * (1.0 - g))
            for n in columns:
                po[rows, n] = (
                    x[rows, n].astype(F32)
                    + jnp.dot(gat[rows, :], w2[:, n], preferred_element_type=F32)
                ).astype(BF16)

            @pl.when(i == 0)
            def _():
                pl.semaphore_wait(barrier, 10)

            @pl.when(s < 3)
            def _():
                send_x(m).start()

            @pl.when(s < 2)
            def _():
                for n in columns:
                    sk[rows, n] = jnp.dot(
                        po[rows, :], w3[:, n], preferred_element_type=F32
                    ).astype(BF16)

                @pl.when(s == 1)
                def _():
                    send_sk(m).start()

                    @pl.when(m == 1)
                    def _():
                        for j in range(2):
                            send_x(j).wait_send()
                            send_sk(j).wait_send()
                        pl.semaphore_signal(turn, inc=1, device_id={"segment": 0}, device_id_type=MESH)

                @pl.when(s == 0)
                def _():
                    @pl.when(m == 1)
                    def _():
                        pl.semaphore_wait(turn, 1)

                    send_sk(m).start()

        @pl.when(kind == 1)
        def _():
            @pl.when((s == 3) & (m == 0))
            def _():
                up_load.wait()

            @pl.when(s < 2)
            def _():
                send_dk(m).wait_recv()
                for n in columns:
                    acc[:, n] = jnp.dot(dk[rows, :], wt[2, :, n], preferred_element_type=F32)

                @pl.when((m == 1) & (s < 2))
                def _():
                    product(dk)

            @pl.when(s < 3)
            def _():
                send_up(m).wait_recv()

            @pl.when(s < 2)
            def _():
                tot[rows, :] = (up[rows, :].astype(F32) + acc[...]).astype(BF16)

            @pl.when(s >= 2)
            def _():
                tot[rows, :] = up[rows, :]

            for n in columns:
                dpre[rows, n] = (
                    jnp.dot(tot[rows, :], wt[1, :, n], preferred_element_type=F32)
                    * pre[rows, n]
                ).astype(BF16)

            @pl.when(s == 0)
            def _():
                swap(1, m)
                swap(0, m)

            @pl.when(s == 2)
            def _():
                for n in columns:
                    dk[rows, n] = jnp.dot(
                        dpre[rows, :], wt[2, :, n], preferred_element_type=F32
                    ).astype(BF16)
                send_dk(m).start()

            for n in columns:
                gi[rows, n] = (
                    tot[rows, n].astype(F32)
                    + jnp.dot(dpre[rows, :], wt[0, :, n], preferred_element_type=F32)
                ).astype(BF16)

            @pl.when(s > 0)
            def _():
                send_up(m).start()

            @pl.when(s == 3)
            def _():
                for n in columns:
                    dk[rows, n] = jnp.dot(
                        dpre[rows, :], wt[2, :, n], preferred_element_type=F32
                    ).astype(BF16)
                send_dk(m).start()

            @pl.when(s > 0)
            def _():
                swap(1, m)
                swap(0, m)

        @pl.when(kind == on3)
        def _():
            for n in columns:
                left[0, n, slot(0, m)] = x[rows, n].T
                left[1, n, slot(1, m)] = gat[rows, n].T
            for job in range(2):
                for d in range(2):
                    spread(job, m, d).start()

            @pl.when(s < 2)
            def _():
                for n in columns:
                    lt[n, rows] = po[rows, n].T

            @pl.when(s >= 2)
            def _():
                for n in columns:
                    lt[n, rows] = sk[rows, n].T

        @pl.when(i == 1 + 2 * on3)
        def _():
            forward(0)

        @pl.when(((i == 1) & (s < 2)) | ((i == 2) & (s == 2)))
        def _():
            forward(1)

    @pl.when(s == 3)
    def _():
        forward(1)

    @pl.when(s >= 2)
    def _():
        product(dpre)

    def gathered(job):
        for m in range(2):
            for d in range(2):
                relay(job, m, d).wait_recv()
            for by in (1, 2, 3):
                turned(job, m, by).wait_recv()

    def relayed():
        for block in BLOCKS:
            _, col, width, colour, by = block
            cols = pl.ds(col, width)
            first(block, 0).wait_recv()
            r1[:, :, cols] = (
                r1[:, :, cols].astype(F32) + piece(block, here[colour] + by + 4)[...].astype(F32)
            ).astype(BF16)
            first(block, 1).start()

    @pl.when(s < 2)
    def _():
        relayed()

    gathered(1)
    block_product(1)
    gathered(0)
    block_product(0)
    for job in (1, 0):
        for half in range(2):
            o = pl.ds(2 * half, 2)
            sums(job, half, 0).wait_recv()
            pos = (here[1 - job] + 5 - 2 * half) % 4
            p1[job, o] = (p1[job, o].astype(F32) + part[job, o, pos].astype(F32)).astype(BF16)
            sums(job, half, 1).start()
    @pl.when(s >= 2)
    def _():
        relayed()

    for job in (1, 0):
        for half in range(2):
            sums(job, half, 1).wait_recv()
            sums(job, half, 2).wait_recv()
            for o in (2 * half, 2 * half + 1):
                total = (
                    part[job, o, here[1 - job]].astype(F32)
                    + p2[job, o].astype(F32)
                    + p3[job, o].astype(F32)
                )
                lanes = pl.ds(o % 2 * Q, Q)
                hs[job, 0, half, :, lanes] = total[:, :Q].astype(BF16)
                hs[job, 1, half, :, lanes] = total[:, Q:].astype(BF16)
        pair(job).start()
    for block in BLOCKS:
        _, col, width, colour, by = block
        cols = pl.ds(col, width)
        first(block, 1).wait_recv()
        first(block, 2).wait_recv()
        s1[:, :, cols] = (
            piece(block, here[colour])[...].astype(F32)
            + r2[:, :, cols].astype(F32)
            + r3[:, :, cols].astype(F32)
        ).astype(BF16)
        second(block, 0).start()
        second(block, 2).start()
    for block in BLOCKS:
        _, col, width, colour, by = block
        cols = pl.ds(col, width)
        second(block, 0).wait_recv()
        pos = (here[1 - colour] + by + 4) % 4
        q1[:, cols] = (q1[:, cols].astype(F32) + s1[pos, :, cols].astype(F32)).astype(BF16)
        second(block, 1).start()
    for job in (1, 0):
        pair(job).wait_recv()
        for o in range(4):
            lanes = pl.ds(o % 2 * Q, Q)
            mine = hs[job, xh, o // 2, :, lanes].astype(F32)
            fs[job, o, :, :Q] = (mine + hr[job, o // 2, :, lanes].astype(F32)).astype(BF16)
            fs[job, o, :, Q:] = jnp.zeros((40, WIDE - Q), BF16)
        for by in (1, 3, 2):
            last(job, by).start()
        fr[job, here[job]] = fs[job, here[job]]
    for block in BLOCKS:
        _, col, width, colour, by = block
        cols = pl.ds(col, width)
        second(block, 1).wait_recv()
        second(block, 2).wait_recv()
        total = (
            s1[here[1 - colour], :, cols].astype(F32)
            + q2[:, cols].astype(F32)
            + q3[:, cols].astype(F32)
        )
        xs[0, :, cols] = total[:40].astype(BF16)
        xs[1, :, cols] = total[40:].astype(BF16)
    pair(2).start()
    for job in (1, 0):
        for by in (1, 2, 3):
            last(job, by).wait_recv()
        for q in range(4):
            (g_in, g_out)[job][:, q * Q : (q + 1) * Q] = fr[job, q, :, :Q].astype(F32)
    pair(2).wait_recv()
    g_skip[...] = xs[xh].astype(F32) + xr[...].astype(F32)
    for block in BLOCKS:
        for msg in range(3):
            first(block, msg).wait_send()
            second(block, msg).wait_send()
    for k in range(3):
        pair(k).wait_send()
    for job in range(2):
        for n in range(3):
            last(job, n + 1).wait_send()
            for m in range(2):
                turned(job, m, n + 1).wait_send()
                sums(job, m, n).wait_send()
        for m in range(2):
            for d in range(2):
                spread(job, m, d).wait_send()
                relay(job, m, d).wait_send()
    for m in range(2):

        @pl.when((s == 0) | (s == 2))
        def _():
            send_x(m).wait_send()

        @pl.when(s == 0)
        def _():
            send_sk(m).wait_send()

        @pl.when(s > 0)
        def _():
            send_up(m).wait_send()

        @pl.when(s >= 2)
        def _():
            send_dk(m).wait_send()


def deliver(*refs):
    sem = refs[-1]
    copies = [pltpu.make_async_copy(refs[n], refs[5 + n], sem.at[n]) for n in range(5)]
    for copy in copies:
        copy.start()
    for copy in copies:
        copy.wait()


def body(latents, cotangent, timesteps, time_table, w_in, w_out, w_skip):
    rows = 2 * R
    vmem = pl.BlockSpec(memory_space=pltpu.VMEM)
    hbm = pl.BlockSpec(memory_space=pltpu.HBM)
    act = pltpu.VMEM((rows, C), BF16)
    weight = pltpu.VMEM((C, C), BF16)
    quarter = pltpu.VMEM((4, 80, C), BF16)
    sixteenth = pltpu.VMEM((80, C), BF16)
    sums = pltpu.VMEM((2, 4, 40, 2 * Q), BF16)
    halves = pltpu.VMEM((2, 4, 40, WIDE), BF16)
    dma = pltpu.SemaphoreType.DMA
    out_act = jax.ShapeDtypeStruct((rows, C), BF16)
    out_grad = jax.ShapeDtypeStruct((40, C), F32)
    outs = (out_act, out_act, out_grad, out_grad, out_grad)
    results = pl.pallas_call(
        kernel,
        name="window",
        out_shape=outs,
        in_specs=[hbm, hbm, pl.BlockSpec(memory_space=pltpu.SMEM), hbm, hbm, hbm, hbm],
        out_specs=[vmem] * 5,
        scratch_shapes=[
            weight, weight, weight,
            pltpu.VMEM((3, C, C), BF16),
            pltpu.VMEM((1000, C), BF16),
            pltpu.VMEM((2, 1, C), F32),
            pltpu.VMEM((R, C), F32),
            act, act, act, act,
            pltpu.VMEM((rows, C), F32),
            act, act, act,
            pltpu.VMEM((C, rows), BF16),
            pltpu.VMEM((4, 4, 80, C), BF16),
            quarter, quarter, quarter, quarter,
            sixteenth, sixteenth, sixteenth,
            pltpu.VMEM((2, 40, C), BF16),
            pltpu.VMEM((40, C), BF16),
            pltpu.VMEM((2, C, 4 * rows), BF16),
            pltpu.VMEM((2, 4, rows, WIDE), BF16),
            pltpu.VMEM((2, 4 * rows, WIDE), BF16),
            pltpu.VMEM((2, 4, 4, 40, 2 * Q), BF16),
            sums, sums, sums,
            pltpu.VMEM((2, 2, 2, 40, 2 * Q), BF16),
            pltpu.VMEM((2, 2, 40, 2 * Q), BF16),
            halves, halves,
            dma((4,)),
            pltpu.SemaphoreType.REGULAR,
            dma((2,)), dma((3,)),
            dma((2,)), dma((2,)),
            dma((2,)), dma((3,)),
            dma((2,)), dma((2,)),
            dma((2, 3, 4)), dma((2, 3, 4)),
            dma((3,)), dma((3,)),
            dma((2, 2, 2)), dma((2, 2, 2)),
            dma((2, 2, 2)), dma((2, 2, 2)),
            dma((2, 2, 3)), dma((2, 2, 3)),
            dma((2, 2, 3)), dma((2, 2, 3)),
            dma((2, 3)), dma((2, 3)),
        ],
        compiler_params=pltpu.CompilerParams(
            collective_id=0, has_side_effects=True, vmem_limit_bytes=54_000_000
        ),
    )(
        latents.reshape(rows, C), cotangent.reshape(rows, C), timesteps.reshape(2), time_table.reshape(1000, C),
        w_in.reshape(C, C), w_out.reshape(C, C), w_skip.reshape(C, C),
    )
    po, gi, g_in, g_out, g_skip = pl.pallas_call(
        deliver,
        name="deliver",
        out_shape=outs,
        in_specs=[vmem] * 5,
        out_specs=[hbm] * 5,
        scratch_shapes=[dma((5,))],
        compiler_params=pltpu.CompilerParams(vmem_limit_bytes=4_000_000),
    )(*results)
    return (
        po.reshape(1, 2, R, C),
        gi.reshape(1, 2, R, C),
        g_in[None],
        g_out[None],
        g_skip[None],
    )


def solution(mesh):
    in_specs = (
        P(None, "dp", None),
        P(None, "dp", None),
        P(None, "dp"),
        P("segment", None, None),
        P("segment", None, None),
        P("segment", None, None),
        P("segment", None, None),
    )
    out_specs = (
        P("segment", None, "dp", None),
        P("segment", None, "dp", None),
        P("segment", "dp", None),
        P("segment", "dp", None),
        P("segment", "dp", None),
    )
    return jax.shard_map(body, mesh=mesh, in_specs=in_specs, out_specs=out_specs, check_vma=False)
```
